32 devices in a mesh: brick: 8 (over y, x, core), kvec: 4 (over z).
Axes of the slice: x: 2, y: 2, z: 4, core: 2. Of those that a mesh axis runs over, the one named last changes fastest.
Arguments:
- positions: float32 [2, 3, 1024], P(None, None, 'brick'), may hold values from -20 to 20
- moments: float32 [1024, 640], P('brick'), may hold values from -4 to 4
- adj_pos: float32 [3, 1024], P(None, 'brick'), may hold values from -1.8 to 1.8
- final_momentum_adjoint: float32 [3, 1024], P(None, 'brick'), may hold values from -6 to 6
- species: int32 [1024], P('brick'), may hold values from 0 to 5
- masses: float32 [6], replicated, may hold values from 1 to 16
- kint: int32 [1536, 3], P('kvec'), may hold values from -5 to 5
Outputs:
- pos_adjoint: float32 [3, 1024], P(None, 'brick')
- initial_momentum_adjoint: float32 [3, 1024], P(None, 'brick')
The draws below stay inside these ranges and needn't reach their ends.
All inputs are finite; a program needn't handle non-finite values.
Results may differ from the reference program's by a relative error of at most 0.0003.
Values sent between devices are 32-bit elements; how exact they have to be, the bound alone decides.
A program may use at most 64 MiB of HBM per device.

```python
import math
import jax
import jax.numpy as jnp
from jax import lax

C = 64
K = 1536
MOM = 10
NSPEC = 6
STEPS = 2
A_DEV = 128
ATOMS = 1024
N_BRICK = 8


def set_ends(values, key, low, top_value):
    dims = values.shape
    place = [jax.random.randint(jax.random.fold_in(key, axis), (), 0, dims[axis]) for axis in range(len(dims))]
    values = values.at[tuple(place)].set(low)
    longest = dims.index(max(dims))
    place[longest] = (place[longest] + 1) % dims[longest]
    return values.at[tuple(place)].set(top_value)


def levels(own_key, extent, pieces, smallest, high):
    def one(dim, parts):
        steps = jax.random.uniform(jax.random.fold_in(jax.random.fold_in(own_key, 6), dim), (parts,), jnp.float32, smallest / len(pieces), high / len(pieces))
        return jnp.repeat(jnp.exp(steps), extent[dim] // parts).reshape((-1,) + (1,) * (len(extent) - dim - 1))

    loudness = one(*pieces[0])
    for cut in pieces[1:]:
        loudness = loudness * one(*cut)
    return loudness


def noise(stream_key, dims, scale, limit, shards=(), kind=jnp.bfloat16):
    values = jax.random.normal(stream_key, dims, jnp.float32) * scale
    if len(shards) > 0:
        values = levels(stream_key, dims, shards, -0.22, 0.18) * values
    return jnp.clip(values, min=-limit, max=limit).astype(kind)


def setup_inputs(seed: int = 0) -> dict:
    key_list = jax.random.split(jax.random.key(seed), 8)
    positions = jnp.clip(jax.random.uniform(key_list[0], (STEPS, 3, ATOMS), jnp.float32, -20.0, 20.0) * levels(key_list[0], (STEPS, 3, ATOMS), ((2, 8),), -0.4, 0.0), -20.0, 20.0)
    moments = noise(key_list[1], (ATOMS, MOM * C), 0.3, 4.0, ((0, 8),), jnp.float32)
    adj_pos = noise(key_list[2], (3, ATOMS), 0.3, 1.8, ((1, 8),), jnp.float32)
    final_momentum_adjoint = noise(key_list[3], (3, ATOMS), 1.0, 6.0, ((1, 8),), jnp.float32)
    species = set_ends(jax.random.randint(key_list[4], (ATOMS,), 0, NSPEC), jax.random.fold_in(key_list[4], 1), 0, NSPEC - 1).astype(jnp.int32)
    masses = jnp.clip(jnp.exp(jax.random.uniform(key_list[5], (NSPEC,), jnp.float32, math.log(1.0), math.log(16.0))), 1.0, 16.0)
    kint = set_ends(jax.random.randint(key_list[6], (K, 3), -5, 6), jax.random.fold_in(key_list[6], 1), -5, 5).astype(jnp.int32)
    return {"positions": positions, "moments": moments, "adj_pos": adj_pos, "final_momentum_adjoint": final_momentum_adjoint, "species": species, "masses": masses, "kint": kint}


exact = lax.Precision.HIGHEST
wavevector_scale = 0.5
time_step = 0.5
energy_scale = 0.125

def coef_arrays(wavevector_phase):
    kx, ky, kz = (wavevector_phase[:, 0], wavevector_phase[:, 1], wavevector_phase[:, 2])
    ones = jnp.ones_like(kx)
    zeros = jnp.zeros_like(kx)
    acoef = jnp.stack([ones, zeros, zeros, zeros, -0.5 * kx * kx, -0.5 * ky * ky, -0.5 * kz * kz, -kx * ky, -kx * kz, -ky * kz], 1)
    bcoef = jnp.stack([zeros, kx, ky, kz, zeros, zeros, zeros, zeros, zeros, zeros], 1)
    return (acoef, bcoef)

def moment_sums(cos_w, sin_w, moments, acoef, bcoef):
    channels = moments.shape[1] // 10
    cos_part = jnp.dot(cos_w, moments, precision=exact).reshape(cos_w.shape[0], 10, channels)
    sine_component = jnp.dot(sin_w, moments, precision=exact).reshape(cos_w.shape[0], 10, channels)
    real_sum = jnp.einsum('km,kmc->kc', acoef, cos_part, precision=exact) - jnp.einsum('km,kmc->kc', bcoef, sine_component, precision=exact)
    imag_sum = jnp.einsum('km,kmc->kc', acoef, sine_component, precision=exact) + jnp.einsum('km,kmc->kc', bcoef, cos_part, precision=exact)
    return (real_sum, imag_sum)

def weave_terms(leading_dimension, trailing, acoef, bcoef):
    woven = leading_dimension[:, None, :] * acoef[:, :, None] + trailing[:, None, :] * bcoef[:, :, None]
    return woven.reshape(leading_dimension.shape[0], -1)

def tangent_force(wavevector_phase, k_weight, acoef, bcoef, factor, tangent, cosines, sines, k_dot_dir, moments, prefactor):
    factor_re, factor_im = factor
    tangent_re, tangent_im = tangent
    stacked = jnp.stack([weave_terms(tangent_im, -tangent_re, acoef, bcoef), weave_terms(tangent_re, tangent_im, acoef, bcoef), weave_terms(factor_re, factor_im, acoef, bcoef), weave_terms(factor_im, -factor_re, acoef, bcoef)])
    projected = jnp.einsum('jkf,af->jka', stacked, moments, precision=exact)
    inner_sum = cosines * projected[0] - sines * projected[1] - k_dot_dir * (cosines * projected[2] + sines * projected[3])
    return jnp.dot((k_weight[:, None] * wavevector_phase).T, inner_sum, precision=exact) * prefactor

def reference(positions, moments, adj_pos, final_momentum_adjoint, species, masses, kint):
    wavevector_phase = kint.astype(jnp.float32) * wavevector_scale
    ksq = lax.optimization_barrier(jnp.sum(wavevector_phase * wavevector_phase, 1))
    k_weight = jnp.exp(-ksq / 4.0) / jnp.maximum(ksq, 1.0)
    acoef, bcoef = coef_arrays(wavevector_phase)
    prefactor = energy_scale / math.sqrt(ATOMS)
    onehot = (species[None, :] == jnp.arange(NSPEC, dtype=jnp.int32)[:, None]).astype(jnp.float32)
    inv_mass = jnp.dot(1.0 / masses, onehot, precision=exact)
    mom_blocks = moments.reshape(N_BRICK, A_DEV, MOM * C)
    for step_index in reversed(range(STEPS)):
        pos_blocks = positions[step_index].reshape(3, N_BRICK, A_DEV).transpose(1, 0, 2)
        direction = final_momentum_adjoint * inv_mass
        dir_blocks = direction.reshape(3, N_BRICK, A_DEV).transpose(1, 0, 2)

        def block_phases(pos_b, dir_b):
            phase = jnp.dot(wavevector_phase, pos_b, precision=exact)
            return (jnp.cos(phase), jnp.sin(phase), jnp.dot(wavevector_phase, dir_b, precision=exact))

        def add_block(carry, item):
            pos_b, mom_b, dir_b = item
            cosines, sines, k_dot_dir = block_phases(pos_b, dir_b)
            f_re, f_im = moment_sums(cosines, sines, mom_b, acoef, bcoef)
            t_re, t_im = moment_sums(k_dot_dir * cosines, k_dot_dir * sines, mom_b, acoef, bcoef)
            return ((carry[0] + f_re, carry[1] + f_im, carry[2] - t_im, carry[3] + t_re), None)
        zeros = jnp.zeros((K, C), jnp.float32)
        totals, _ = lax.scan(add_block, (zeros, zeros, zeros, zeros), (pos_blocks, mom_blocks, dir_blocks))

        def block_force(item):
            pos_b, mom_b, dir_b = item
            cosines, sines, k_dot_dir = block_phases(pos_b, dir_b)
            return tangent_force(wavevector_phase, k_weight, acoef, bcoef, (totals[0], totals[1]), (totals[2], totals[3]), cosines, sines, k_dot_dir, mom_b, prefactor)
        forces = lax.map(block_force, (pos_blocks, mom_blocks, dir_blocks))
        force = forces.transpose(1, 0, 2).reshape(3, ATOMS)
        adj_pos = adj_pos - time_step * force
        final_momentum_adjoint = final_momentum_adjoint + time_step * adj_pos
    return (adj_pos, final_momentum_adjoint)
```

```python
import functools
import math

import jax
import jax.numpy as jnp
from jax import lax
from jax.experimental import pallas as pl
from jax.experimental.pallas import tpu as pltpu
from jax.sharding import PartitionSpec as P

exact = lax.Precision.HIGHEST
wavevector_scale = 0.5
time_step = 0.5
energy_scale = 0.125


def coef_arrays(wavevector_phase):
    kx, ky, kz = (wavevector_phase[:, 0], wavevector_phase[:, 1], wavevector_phase[:, 2])
    ones = jnp.ones_like(kx)
    zeros = jnp.zeros_like(kx)
    acoef = jnp.stack(
        [
            ones,
            zeros,
            zeros,
            zeros,
            -0.5 * kx * kx,
            -0.5 * ky * ky,
            -0.5 * kz * kz,
            -kx * ky,
            -kx * kz,
            -ky * kz,
        ],
        1,
    )
    bcoef = jnp.stack([zeros, kx, ky, kz, zeros, zeros, zeros, zeros, zeros, zeros], 1)
    return (acoef, bcoef)


def moment_sums(cos_w, sin_w, moments, acoef, bcoef):
    channels = moments.shape[1] // 10
    cos_part = jnp.dot(cos_w, moments, precision=exact).reshape(cos_w.shape[0], 10, channels)
    sine_component = jnp.dot(sin_w, moments, precision=exact).reshape(cos_w.shape[0], 10, channels)
    real_sum = jnp.einsum("km,kmc->kc", acoef, cos_part, precision=exact) - jnp.einsum(
        "km,kmc->kc", bcoef, sine_component, precision=exact
    )
    imag_sum = jnp.einsum("km,kmc->kc", acoef, sine_component, precision=exact) + jnp.einsum(
        "km,kmc->kc", bcoef, cos_part, precision=exact
    )
    return (real_sum, imag_sum)


def weave_terms(leading_dimension, trailing, acoef, bcoef):
    woven = (
        leading_dimension[:, None, :] * acoef[:, :, None] + trailing[:, None, :] * bcoef[:, :, None]
    )
    return woven.reshape(leading_dimension.shape[0], -1)


def tangent_force(
    wavevector_phase,
    k_weight,
    acoef,
    bcoef,
    factor,
    tangent,
    cosines,
    sines,
    k_dot_dir,
    moments,
    prefactor,
):
    factor_re, factor_im = factor
    tangent_re, tangent_im = tangent
    stacked = jnp.stack(
        [
            weave_terms(tangent_im, -tangent_re, acoef, bcoef),
            weave_terms(tangent_re, tangent_im, acoef, bcoef),
            weave_terms(factor_re, factor_im, acoef, bcoef),
            weave_terms(factor_im, -factor_re, acoef, bcoef),
        ]
    )
    projected = jnp.einsum("jkf,af->jka", stacked, moments, precision=exact)
    inner_sum = (
        cosines * projected[0]
        - sines * projected[1]
        - k_dot_dir * (cosines * projected[2] + sines * projected[3])
    )
    return jnp.dot((k_weight[:, None] * wavevector_phase).T, inner_sum, precision=exact) * prefactor


def plain_local(positions, moments, adj_pos, final_momentum_adjoint, species, masses, kint):
    wavevector_phase = kint.astype(jnp.float32) * wavevector_scale
    ksq = jnp.sum(wavevector_phase * wavevector_phase, 1)
    k_weight = jnp.exp(-ksq / 4.0) / jnp.maximum(ksq, 1.0)
    acoef, bcoef = coef_arrays(wavevector_phase)
    prefactor = energy_scale / math.sqrt(positions.shape[2] * lax.axis_size("brick"))
    onehot = (species[None, :] == jnp.arange(masses.shape[0], dtype=jnp.int32)[:, None]).astype(
        jnp.float32
    )
    inv_mass = jnp.dot(1.0 / masses, onehot, precision=exact)
    num_steps = positions.shape[0]

    def step_phases(step_index):
        phase = jnp.dot(wavevector_phase, positions[step_index], precision=exact)
        return (jnp.cos(phase), jnp.sin(phase))

    phase_list = [step_phases(step_index) for step_index in range(num_steps)]
    for step_index in reversed(range(num_steps)):
        cosines, sines = phase_list[step_index]
        direction = final_momentum_adjoint * inv_mass
        k_dot_dir = jnp.dot(wavevector_phase, direction, precision=exact)
        tangent_real_part, tan_im = moment_sums(
            k_dot_dir * cosines, k_dot_dir * sines, moments, acoef, bcoef
        )
        fac_re, fac_im = moment_sums(cosines, sines, moments, acoef, bcoef)
        summed_terms = lax.psum((fac_re, fac_im, -tan_im, tangent_real_part), "brick")
        factor = (summed_terms[0], summed_terms[1])
        tangent = (summed_terms[2], summed_terms[3])
        partial_force = tangent_force(
            wavevector_phase,
            k_weight,
            acoef,
            bcoef,
            factor,
            tangent,
            cosines,
            sines,
            k_dot_dir,
            moments,
            prefactor,
        )
        force = lax.psum(partial_force, "kvec")
        adj_pos = adj_pos - time_step * force
        final_momentum_adjoint = final_momentum_adjoint + time_step * adj_pos
    return (adj_pos, final_momentum_adjoint)


def plain(mesh):
    placed = (
        P(None, None, "brick"),
        P("brick", None),
        P(None, "brick"),
        P(None, "brick"),
        P("brick"),
        P(),
        P("kvec", None),
    )
    return jax.shard_map(
        plain_local,
        mesh=mesh,
        in_specs=placed,
        out_specs=(P(None, "brick"), P(None, "brick")),
        check_vma=False,
    )


MESH = pl.DeviceIdType.MESH
GROUP = 8
MOM = 10
LANES = 128
F32, BF16 = jnp.float32, jnp.bfloat16
two_over_pi = 2.0 / math.pi
half_pi_parts = (1.5703125, 4.837512969970703125e-4, 7.549789948768648e-8)


def sin_cos(phase):
    n = jnp.round(phase * two_over_pi)
    r = phase - n * half_pi_parts[0]
    r = r - n * half_pi_parts[1]
    r = r - n * half_pi_parts[2]
    q = n.astype(jnp.int32)
    z = r * r
    s = r + r * z * (-1.6666654611e-1 + z * (8.3321608736e-3 + z * -1.9515295891e-4))
    c = 1.0 - 0.5 * z + z * z * (
        4.166664568298827e-2 + z * (-1.388731625493765e-3 + z * 2.443315711809948e-5)
    )
    odd = (q & 1) == 1
    sine = jnp.where(odd, c, s)
    cosine = jnp.where(odd, s, c)
    sine = jnp.where((q & 2) == 2, -sine, sine)
    cosine = jnp.where(((q + 1) & 2) == 2, -cosine, cosine)
    return sine, cosine


def split(x):
    high = x.astype(BF16)
    return high, (x - high.astype(F32)).astype(BF16)


def wide(x, copies):
    return jnp.concatenate([x] * copies, axis=1)


def fold(x):
    out = x[0:8]
    for row in range(8, x.shape[0], 8):
        out = out + x[row : row + 8]
    return out


def spread(x):
    for shift in (8, 16, 32, 64):
        x = x + pltpu.roll(x, shift, 1)
    return x


def kernel(
    kvecs,
    prefactor,
    pos_ref,
    mom_ref,
    adj_ref,
    fma_ref,
    spec_ref,
    mass_ref,
    kint_ref,
    out_adj,
    out_fma,
    pack,
    landed,
    flown,
    rows,
    sent,
    qall,
    kmap,
    amap,
    w1,
    w2,
    trig,
    high,
    low,
    sums,
    proj,
    acc,
    part,
    bricks,
    total,
    zs,
    fresh,
    dirs,
    send_sem,
    recv_sem,
    zsend_sem,
    zrecv_sem,
):
    me = lax.axis_index("brick")
    mev = lax.axis_index("kvec")
    atoms = LANES * GROUP
    kdev = kint_ref.shape[0]
    steps = pos_ref.shape[0]

    def ahead(off):
        return lax.rem(me + off, GROUP)

    def behind(off):
        return lax.rem(me + GROUP - off, GROUP)

    def brick_copy(phase, off, src, dst, target):
        return pltpu.make_async_remote_copy(
            src_ref=src,
            dst_ref=dst,
            send_sem=send_sem.at[phase, off],
            recv_sem=recv_sem.at[phase, off],
            device_id=(target, mev),
            device_id_type=MESH,
        )

    barrier = pltpu.get_barrier_semaphore()
    for off in range(1, GROUP):
        pl.semaphore_signal(barrier, inc=1, device_id=(ahead(off), mev), device_id_type=MESH)
    for off in range(1, kvecs):
        pl.semaphore_signal(
            barrier, inc=1, device_id=(me, lax.rem(mev + off, kvecs)), device_id_type=MESH
        )

    species = spec_ref[...]
    mass = jnp.zeros(species.shape, F32)
    for kind in range(mass_ref.shape[0]):
        mass = jnp.where(species == kind, mass_ref[kind], mass)
    inv_mass = 1.0 / mass
    pack[...] = jnp.zeros_like(pack)
    for step in range(steps):
        pack[3 * step : 3 * step + 3, :] = pos_ref[step]
    pack[3 * steps : 3 * steps + 3, :] = fma_ref[...] * inv_mass
    for piece in range(mom_ref.shape[1] // LANES):
        turned = mom_ref[:, piece * LANES : (piece + 1) * LANES].T
        sent[2 * piece : 2 * piece + 2] = turned.reshape(2, GROUP, 8, LANES)

    pl.semaphore_wait(barrier, GROUP - 1 + kvecs - 1)
    copies = []
    for off in range(1, GROUP):
        copies.append(
            brick_copy(0, off, pack, landed.at[off], ahead(off))
        )
        copies[-1].start()
    for off in range(1, GROUP):
        copies.append(
            brick_copy(
                1,
                off,
                sent.at[:, ahead(off)],
                qall.at[off],
                ahead(off),
            )
        )
        copies[-1].start()
    rows[:, 0:LANES] = pack[...]

    wave = kint_ref[...].astype(F32) * wavevector_scale
    kx = jnp.broadcast_to(wave[:, 0:1], (kdev, LANES))
    ky = jnp.broadcast_to(wave[:, 1:2], (kdev, LANES))
    kz = jnp.broadcast_to(wave[:, 2:3], (kdev, LANES))
    ksq = kx * kx + ky * ky + kz * kz
    weight = jnp.exp(-ksq / 4.0) / jnp.maximum(ksq, 1.0) * prefactor
    for axis, k in enumerate((kx, ky, kz)):
        kmap[axis] = k
        kmap[3 + axis] = weight * k
    lane = lax.broadcasted_iota(jnp.int32, (1, LANES), 1)
    used = MOM * 8

    def maps(component):
        def among(*names):
            out = component == names[0]
            for name in names[1:]:
                out = out | (component == name)
            return out

        one, none = jnp.ones((1, LANES), F32), jnp.zeros((1, LANES), F32)
        scale_a = jnp.where(component == 0, one, none)
        scale_a = jnp.where(among(4, 5, 6), -0.5 * one, scale_a)
        scale_a = jnp.where(among(7, 8, 9), -one, scale_a)
        scale_b = jnp.where(among(1, 2, 3), one, none)
        first = jnp.where(
            among(1, 4, 7, 8), kx, jnp.where(among(2, 5, 9), ky, jnp.where(among(3, 6), kz, one))
        )
        second = jnp.where(
            among(4), kx, jnp.where(among(5, 7), ky, jnp.where(among(6, 8, 9), kz, one))
        )
        return first * second * scale_a, first * scale_b

    room = (LANES - used) // 8
    amap[0], amap[1] = maps(jnp.where(lane < used, lane // 8, (lane - used) // 8))
    amap[2], amap[3] = maps(
        jnp.where(
            lane < used,
            lane // 8,
            jnp.where(lane < used + (MOM - room) * 8, room + (lane - used) // 8, MOM),
        )
    )

    for off in range(1, GROUP):
        copies[off - 1].wait_recv()
        rows[:, off * LANES : (off + 1) * LANES] = landed[off]

    tile = 16

    def make_trig(step, first, last):
        @pl.loop(first, last)
        def _(chunk):
            at = pl.multiple_of(chunk * tile, tile)
            phase = 0.0
            for axis in range(3):
                phase += wide(kmap[axis, pl.ds(at, tile)], GROUP) * rows[3 * step + axis, :][None]
            sine, cosine = sin_cos(phase)
            trig[step, 0, pl.ds(at, tile)] = cosine
            trig[step, 1, pl.ds(at, tile)] = sine
            high[step, 0, pl.ds(at, tile)], low[step, 0, pl.ds(at, tile)] = split(cosine)
            high[step, 1, pl.ds(at, tile)], low[step, 1, pl.ds(at, tile)] = split(sine)

    def along(at, rows_here, direction):
        out = 0.0
        for axis in range(3):
            out += wide(kmap[axis, pl.ds(at, rows_here)], GROUP) * direction(axis)
        return out

    def make_tangent(step, direction):
        @pl.loop(0, kdev // tile)
        def _(chunk):
            at = pl.multiple_of(chunk * tile, tile)
            k_dot_dir = along(at, tile, direction)
            for which in range(2):
                moved = k_dot_dir * trig[step, which, pl.ds(at, tile)]
                high[steps, which, pl.ds(at, tile)], low[steps, which, pl.ds(at, tile)] = split(
                    moved
                )

    block = 128

    def make_sums(source, slot):
        @pl.loop(0, kdev // block)
        def _(chunk):
            at = pl.multiple_of(chunk * block, block)
            both = []
            for which in range(2):
                wide_sum = jnp.dot(
                    high[source, which, pl.ds(at, block)], w1[...], preferred_element_type=F32
                )
                rest = jnp.dot(
                    low[source, which, pl.ds(at, block)],
                    w1[:, 0:LANES],
                    preferred_element_type=F32,
                )
                both.append(wide_sum[:, 0:LANES] + wide_sum[:, LANES:] + rest)
            a, b = amap[0, pl.ds(at, block)], amap[1, pl.ds(at, block)]
            sums[slot, 0, pl.ds(at, block)] = spread(a * both[0] - b * both[1])
            sums[slot, 1, pl.ds(at, block)] = spread(a * both[1] + b * both[0])

    def project(real, imag, at):
        one = real * amap[0, pl.ds(at, block)] + imag * amap[1, pl.ds(at, block)]
        two = real * amap[2, pl.ds(at, block)] + imag * amap[3, pl.ds(at, block)]
        top = one.astype(BF16)
        rest = jnp.where(lane < used, one - top.astype(F32), two).astype(BF16)
        return jnp.dot(jnp.concatenate([top, rest], axis=1), w2[...], preferred_element_type=F32)

    def factor_part(step, slot):
        acc[3:9] = jnp.zeros((6, 8, atoms), F32)

        @pl.loop(0, kdev // block)
        def _(chunk):
            at = pl.multiple_of(chunk * block, block)
            real, imag = sums[slot, 0, pl.ds(at, block)], sums[slot, 1, pl.ds(at, block)]
            proj[0] = project(real, imag, at)
            proj[1] = project(imag, -real, at)

            @pl.loop(0, block // tile)
            def _(inner):
                here = pl.multiple_of(inner * tile, tile)
                there = pl.multiple_of(at + here, tile)
                value = (
                    trig[step, 0, pl.ds(there, tile)] * proj[0, pl.ds(here, tile)]
                    + trig[step, 1, pl.ds(there, tile)] * proj[1, pl.ds(here, tile)]
                )
                row = 3
                for axis in range(3):
                    weighted = wide(kmap[3 + axis, pl.ds(there, tile)], GROUP) * value
                    for other in range(axis, 3):
                        acc[row] += fold(wide(kmap[other, pl.ds(there, tile)], GROUP) * weighted)
                        row += 1

    def tangent_part(step, slot):
        acc[0:3] = jnp.zeros((3, 8, atoms), F32)

        @pl.loop(0, kdev // block)
        def _(chunk):
            at = pl.multiple_of(chunk * block, block)
            real, imag = sums[slot, 0, pl.ds(at, block)], sums[slot, 1, pl.ds(at, block)]
            proj[0] = project(real, imag, at)
            proj[1] = project(-imag, real, at)

            @pl.loop(0, block // tile)
            def _(inner):
                here = pl.multiple_of(inner * tile, tile)
                there = pl.multiple_of(at + here, tile)
                value = (
                    trig[step, 0, pl.ds(there, tile)] * proj[0, pl.ds(here, tile)]
                    - trig[step, 1, pl.ds(there, tile)] * proj[1, pl.ds(here, tile)]
                )
                for axis in range(3):
                    acc[axis] += fold(wide(kmap[3 + axis, pl.ds(there, tile)], GROUP) * value)

    def send_force(step, direction):
        summed = [jnp.sum(acc[row], axis=0, keepdims=True) for row in range(9)]
        second = {}
        row = 3
        for axis in range(3):
            for other in range(axis, 3):
                second[axis, other] = second[other, axis] = summed[row]
                row += 1
        part[step] = jnp.zeros((GROUP, 8, LANES), F32)
        for axis in range(3):
            out = summed[axis]
            for other in range(3):
                out = out - second[axis, other] * direction(other)
            for off in range(GROUP):
                part[step, off, axis : axis + 1, :] = out[:, off * LANES : (off + 1) * LANES]
        started = []
        for off in range(1, GROUP):
            started.append(
                brick_copy(
                    2 + step,
                    off,
                    part.at[step, off],
                    bricks.at[step, off],
                    behind(off),
                )
            )
            started[-1].start()
        return started

    def exchange_force(step, started):
        for copy in started:
            copy.wait_recv()
        out = part[step, 0]
        for off in range(1, GROUP):
            out = out + bricks[step, off]
        total[step] = out
        zs[step, 0] = out
        over = []
        for off in range(1, kvecs):
            over.append(
                pltpu.make_async_remote_copy(
                    src_ref=total.at[step],
                    dst_ref=zs.at[step, off],
                    send_sem=zsend_sem.at[step, off],
                    recv_sem=zrecv_sem.at[step, off],
                    device_id=(me, lax.rem(mev + off, kvecs)),
                    device_id_type=MESH,
                )
            )
            over[-1].start()
        return over

    def finish_force(step, over):
        for copy in over:
            copy.wait_recv()
        out = jnp.zeros((8, LANES), F32)
        for owner in range(kvecs):
            off = lax.rem(mev + kvecs - owner, kvecs)
            share = zs[step, 0]
            for other in range(1, kvecs):
                share = jnp.where(off == other, zs[step, other], share)
            out = out + share
        return out[0:3]

    def first_direction(axis):
        return rows[3 * steps + axis, :][None]

    last = steps - 1
    chunks = kdev // tile
    make_trig(last, 0, chunks)
    make_tangent(last, first_direction)
    for off in range(1, GROUP):
        copies[GROUP - 1 + off - 1].wait_recv()
    moments = jnp.concatenate(
        [sent[:, pl.ds(me, 1)].reshape(used, LANES)]
        + [qall[off].reshape(used, LANES) for off in range(1, GROUP)],
        axis=1,
    )
    q_high, q_low = split(moments)
    turned = jnp.concatenate([moments, jnp.zeros((LANES - used, atoms), F32)], axis=0).T
    w1[:, 0:LANES], w1[:, LANES:] = split(turned)
    fits = LANES - used
    w2[0:used] = q_high
    w2[used:LANES] = q_low[0:fits]
    w2[LANES : LANES + used] = q_high
    w2[LANES + used : LANES + 2 * used - fits] = q_low[fits:]
    w2[LANES + 2 * used - fits :] = jnp.zeros((2 * LANES - (LANES + 2 * used - fits), atoms), BF16)

    adj, fma = adj_ref[...], fma_ref[...]
    direction = first_direction
    for step in reversed(range(steps)):
        if step == last:
            make_sums(step, 0)
            factor_part(step, 0)
        make_sums(steps, 1)
        tangent_part(step, 1)
        started = send_force(step, direction)
        if step > 0:
            make_trig(step - 1, 0, chunks // 2)
        over = exchange_force(step, started)
        if step > 0:
            make_trig(step - 1, chunks // 2, chunks)
        force = finish_force(step, over)
        adj = adj - time_step * force
        fma = fma + time_step * adj
        copies += started + over
        if step > 0:
            fresh[step - 1] = jnp.concatenate([fma * inv_mass, jnp.zeros((5, LANES), F32)], axis=0)
            sends = []
            for off in range(1, GROUP):
                sends.append(
                    brick_copy(
                        2 + steps + step - 1,
                        off,
                        fresh.at[step - 1],
                        flown.at[step - 1, off],
                        ahead(off),
                    )
                )
                sends[-1].start()
            dirs[step - 1, :, 0:LANES] = fresh[step - 1]
            make_sums(step - 1, 0)
            factor_part(step - 1, 0)
            for off in range(1, GROUP):
                sends[off - 1].wait_recv()
                dirs[step - 1, :, off * LANES : (off + 1) * LANES] = flown[step - 1, off]
            copies += sends

            def direction(axis, step=step):
                return dirs[step - 1, axis, :][None]

            make_tangent(step - 1, direction)
    out_adj[...] = adj
    out_fma[...] = fma
    for copy in copies:
        copy.wait_send()


def fused(kvecs, bricks, positions, moments, adj_pos, final_momentum_adjoint, species, masses, kint):
    steps, _, here = positions.shape
    kdev = kint.shape[0]
    atoms = here * GROUP
    phases = 2 + 2 * steps - 1
    prefactor = energy_scale / math.sqrt(here * bricks)
    vmem = pl.BlockSpec(memory_space=pltpu.VMEM)
    small = jax.ShapeDtypeStruct((3, here), F32)
    return pl.pallas_call(
        functools.partial(kernel, kvecs, prefactor),
        out_shape=(small, small),
        in_specs=[vmem] * 5 + [pl.BlockSpec(memory_space=pltpu.SMEM), vmem],
        out_specs=(vmem, vmem),
        scratch_shapes=[
            pltpu.VMEM((16, here), F32),
            pltpu.VMEM((GROUP, 16, here), F32),
            pltpu.VMEM((steps, GROUP, 8, here), F32),
            pltpu.VMEM((16, atoms), F32),
            pltpu.VMEM((MOM, GROUP, 8, here), F32),
            pltpu.VMEM((GROUP, MOM, 8, here), F32),
            pltpu.VMEM((6, kdev, LANES), F32),
            pltpu.VMEM((4, kdev, LANES), F32),
            pltpu.VMEM((atoms, 2 * LANES), BF16),
            pltpu.VMEM((2 * LANES, atoms), BF16),
            pltpu.VMEM((steps, 2, kdev, atoms), F32),
            pltpu.VMEM((steps + 1, 2, kdev, atoms), BF16),
            pltpu.VMEM((steps + 1, 2, kdev, atoms), BF16),
            pltpu.VMEM((2, 2, kdev, LANES), F32),
            pltpu.VMEM((2, 128, atoms), F32),
            pltpu.VMEM((9, 8, atoms), F32),
            pltpu.VMEM((steps, GROUP, 8, here), F32),
            pltpu.VMEM((steps, GROUP, 8, here), F32),
            pltpu.VMEM((steps, 8, here), F32),
            pltpu.VMEM((steps, kvecs, 8, here), F32),
            pltpu.VMEM((steps, 8, here), F32),
            pltpu.VMEM((steps, 8, atoms), F32),
            pltpu.SemaphoreType.DMA((phases, GROUP)),
            pltpu.SemaphoreType.DMA((phases, GROUP)),
            pltpu.SemaphoreType.DMA((steps, kvecs)),
            pltpu.SemaphoreType.DMA((steps, kvecs)),
        ],
        compiler_params=pltpu.CompilerParams(
            collective_id=0, has_side_effects=True, vmem_limit_bytes=48 << 20
        ),
    )(
        positions,
        moments,
        adj_pos,
        final_momentum_adjoint,
        species.reshape(1, here),
        masses,
        kint,
    )


def solution(mesh):
    bricks, kvecs = mesh.shape["brick"], mesh.shape["kvec"]
    if bricks != GROUP:
        return plain(mesh)
    placed = (
        P(None, None, "brick"),
        P("brick", None),
        P(None, "brick"),
        P(None, "brick"),
        P("brick"),
        P(),
        P("kvec", None),
    )
    return jax.shard_map(
        functools.partial(fused, kvecs, bricks),
        mesh=mesh,
        in_specs=placed,
        out_specs=(P(None, "brick"), P(None, "brick")),
        check_vma=False,
    )
```

```python
import functools
import math

import jax
import jax.numpy as jnp
from jax import lax
from jax.experimental import pallas as pl
from jax.experimental.pallas import tpu as pltpu
from jax.sharding import PartitionSpec as P

exact = lax.Precision.HIGHEST
wavevector_scale = 0.5
time_step = 0.5
energy_scale = 0.125


def coef_arrays(wavevector_phase):
    kx, ky, kz = (wavevector_phase[:, 0], wavevector_phase[:, 1], wavevector_phase[:, 2])
    ones = jnp.ones_like(kx)
    zeros = jnp.zeros_like(kx)
    acoef = jnp.stack(
        [
            ones,
            zeros,
            zeros,
            zeros,
            -0.5 * kx * kx,
            -0.5 * ky * ky,
            -0.5 * kz * kz,
            -kx * ky,
            -kx * kz,
            -ky * kz,
        ],
        1,
    )
    bcoef = jnp.stack([zeros, kx, ky, kz, zeros, zeros, zeros, zeros, zeros, zeros], 1)
    return (acoef, bcoef)


def moment_sums(cos_w, sin_w, moments, acoef, bcoef):
    channels = moments.shape[1] // 10
    cos_part = jnp.dot(cos_w, moments, precision=exact).reshape(cos_w.shape[0], 10, channels)
    sine_component = jnp.dot(sin_w, moments, precision=exact).reshape(cos_w.shape[0], 10, channels)
    real_sum = jnp.einsum("km,kmc->kc", acoef, cos_part, precision=exact) - jnp.einsum(
        "km,kmc->kc", bcoef, sine_component, precision=exact
    )
    imag_sum = jnp.einsum("km,kmc->kc", acoef, sine_component, precision=exact) + jnp.einsum(
        "km,kmc->kc", bcoef, cos_part, precision=exact
    )
    return (real_sum, imag_sum)


def weave_terms(leading_dimension, trailing, acoef, bcoef):
    woven = (
        leading_dimension[:, None, :] * acoef[:, :, None] + trailing[:, None, :] * bcoef[:, :, None]
    )
    return woven.reshape(leading_dimension.shape[0], -1)


def tangent_force(
    wavevector_phase,
    k_weight,
    acoef,
    bcoef,
    factor,
    tangent,
    cosines,
    sines,
    k_dot_dir,
    moments,
    prefactor,
):
    factor_re, factor_im = factor
    tangent_re, tangent_im = tangent
    stacked = jnp.stack(
        [
            weave_terms(tangent_im, -tangent_re, acoef, bcoef),
            weave_terms(tangent_re, tangent_im, acoef, bcoef),
            weave_terms(factor_re, factor_im, acoef, bcoef),
            weave_terms(factor_im, -factor_re, acoef, bcoef),
        ]
    )
    projected = jnp.einsum("jkf,af->jka", stacked, moments, precision=exact)
    inner_sum = (
        cosines * projected[0]
        - sines * projected[1]
        - k_dot_dir * (cosines * projected[2] + sines * projected[3])
    )
    return jnp.dot((k_weight[:, None] * wavevector_phase).T, inner_sum, precision=exact) * prefactor


def plain_local(positions, moments, adj_pos, final_momentum_adjoint, species, masses, kint):
    wavevector_phase = kint.astype(jnp.float32) * wavevector_scale
    ksq = jnp.sum(wavevector_phase * wavevector_phase, 1)
    k_weight = jnp.exp(-ksq / 4.0) / jnp.maximum(ksq, 1.0)
    acoef, bcoef = coef_arrays(wavevector_phase)
    prefactor = energy_scale / math.sqrt(positions.shape[2] * lax.axis_size("brick"))
    onehot = (species[None, :] == jnp.arange(masses.shape[0], dtype=jnp.int32)[:, None]).astype(
        jnp.float32
    )
    inv_mass = jnp.dot(1.0 / masses, onehot, precision=exact)
    num_steps = positions.shape[0]

    def step_phases(step_index):
        phase = jnp.dot(wavevector_phase, positions[step_index], precision=exact)
        return (jnp.cos(phase), jnp.sin(phase))

    phase_list = [step_phases(step_index) for step_index in range(num_steps)]
    for step_index in reversed(range(num_steps)):
        cosines, sines = phase_list[step_index]
        direction = final_momentum_adjoint * inv_mass
        k_dot_dir = jnp.dot(wavevector_phase, direction, precision=exact)
        tangent_real_part, tan_im = moment_sums(
            k_dot_dir * cosines, k_dot_dir * sines, moments, acoef, bcoef
        )
        fac_re, fac_im = moment_sums(cosines, sines, moments, acoef, bcoef)
        summed_terms = lax.psum((fac_re, fac_im, -tan_im, tangent_real_part), "brick")
        factor = (summed_terms[0], summed_terms[1])
        tangent = (summed_terms[2], summed_terms[3])
        partial_force = tangent_force(
            wavevector_phase,
            k_weight,
            acoef,
            bcoef,
            factor,
            tangent,
            cosines,
            sines,
            k_dot_dir,
            moments,
            prefactor,
        )
        force = lax.psum(partial_force, "kvec")
        adj_pos = adj_pos - time_step * force
        final_momentum_adjoint = final_momentum_adjoint + time_step * adj_pos
    return (adj_pos, final_momentum_adjoint)


def plain(mesh):
    placed = (
        P(None, None, "brick"),
        P("brick", None),
        P(None, "brick"),
        P(None, "brick"),
        P("brick"),
        P(),
        P("kvec", None),
    )
    return jax.shard_map(
        plain_local,
        mesh=mesh,
        in_specs=placed,
        out_specs=(P(None, "brick"), P(None, "brick")),
        check_vma=False,
    )


MESH = pl.DeviceIdType.MESH
GROUP = 8
MOM = 10
LANES = 128
F32, BF16 = jnp.float32, jnp.bfloat16
two_over_pi = 2.0 / math.pi
half_pi_parts = (1.5703125, 4.837512969970703125e-4, 7.549789948768648e-8)


def sin_cos(phase):
    n = jnp.round(phase * two_over_pi)
    r = phase - n * half_pi_parts[0]
    r = r - n * half_pi_parts[1]
    r = r - n * half_pi_parts[2]
    q = n.astype(jnp.int32)
    z = r * r
    s = r + r * z * (-1.6666654611e-1 + z * (8.3321608736e-3 + z * -1.9515295891e-4))
    c = 1.0 - 0.5 * z + z * z * (
        4.166664568298827e-2 + z * (-1.388731625493765e-3 + z * 2.443315711809948e-5)
    )
    odd = (q & 1) == 1
    sine = jnp.where(odd, c, s)
    cosine = jnp.where(odd, s, c)
    sine = jnp.where((q & 2) == 2, -sine, sine)
    cosine = jnp.where(((q + 1) & 2) == 2, -cosine, cosine)
    return sine, cosine


def split(x):
    high = x.astype(BF16)
    return high, (x - high.astype(F32)).astype(BF16)


def wide(x, copies):
    return jnp.concatenate([x] * copies, axis=1)


def fold(x):
    out = x[0:8]
    for row in range(8, x.shape[0], 8):
        out = out + x[row : row + 8]
    return out


def spread(x):
    for shift in (8, 16, 32, 64):
        x = x + pltpu.roll(x, shift, 1)
    return x


def kernel(
    kvecs,
    prefactor,
    pos_ref,
    mom_ref,
    adj_ref,
    fma_ref,
    spec_ref,
    mass_ref,
    kint_ref,
    out_adj,
    out_fma,
    pack,
    landed,
    flown,
    rows,
    sent,
    qall,
    kmap,
    amap,
    w1,
    w2,
    trig,
    high,
    low,
    sums,
    proj,
    acc,
    part,
    bricks,
    fresh,
    dirs,
    send_sem,
    recv_sem,
    zsend_sem,
    zrecv_sem,
):
    me = lax.axis_index("brick")
    mev = lax.axis_index("kvec")
    atoms = LANES * GROUP
    kdev = kint_ref.shape[0]
    steps = pos_ref.shape[0]

    def ahead(off):
        return lax.rem(me + off, GROUP)

    def behind(off):
        return lax.rem(me + GROUP - off, GROUP)

    def brick_copy(phase, off, src, dst, target):
        return pltpu.make_async_remote_copy(
            src_ref=src,
            dst_ref=dst,
            send_sem=send_sem.at[phase, off],
            recv_sem=recv_sem.at[phase, off],
            device_id=(target, mev),
            device_id_type=MESH,
        )

    barrier = pltpu.get_barrier_semaphore()
    for over in range(kvecs):
        for off in range(GROUP):
            if over > 0 or off > 0:
                pl.semaphore_signal(
                    barrier,
                    inc=1,
                    device_id=(ahead(off), lax.rem(mev + over, kvecs)),
                    device_id_type=MESH,
                )

    species = spec_ref[...]
    mass = jnp.zeros(species.shape, F32)
    for kind in range(mass_ref.shape[0]):
        mass = jnp.where(species == kind, mass_ref[kind], mass)
    inv_mass = 1.0 / mass
    pack[...] = jnp.zeros_like(pack)
    for step in range(steps):
        pack[3 * step : 3 * step + 3, :] = pos_ref[step]
    pack[3 * steps : 3 * steps + 3, :] = fma_ref[...] * inv_mass
    for piece in range(mom_ref.shape[1] // LANES):
        turned = mom_ref[:, piece * LANES : (piece + 1) * LANES].T
        sent[2 * piece : 2 * piece + 2] = turned.reshape(2, GROUP, 8, LANES)

    pl.semaphore_wait(barrier, GROUP * kvecs - 1)
    copies = []
    for off in range(1, GROUP):
        copies.append(
            brick_copy(0, off, pack, landed.at[off], ahead(off))
        )
        copies[-1].start()
    for off in range(1, GROUP):
        copies.append(
            brick_copy(
                1,
                off,
                sent.at[:, ahead(off)],
                qall.at[off],
                ahead(off),
            )
        )
        copies[-1].start()
    rows[:, 0:LANES] = pack[...]

    wave = kint_ref[...].astype(F32) * wavevector_scale
    kx = jnp.broadcast_to(wave[:, 0:1], (kdev, LANES))
    ky = jnp.broadcast_to(wave[:, 1:2], (kdev, LANES))
    kz = jnp.broadcast_to(wave[:, 2:3], (kdev, LANES))
    ksq = kx * kx + ky * ky + kz * kz
    weight = jnp.exp(-ksq / 4.0) / jnp.maximum(ksq, 1.0) * prefactor
    for axis, k in enumerate((kx, ky, kz)):
        kmap[axis] = k
        kmap[3 + axis] = weight * k
    lane = lax.broadcasted_iota(jnp.int32, (1, LANES), 1)
    used = MOM * 8

    def maps(component):
        def among(*names):
            out = component == names[0]
            for name in names[1:]:
                out = out | (component == name)
            return out

        one, none = jnp.ones((1, LANES), F32), jnp.zeros((1, LANES), F32)
        scale_a = jnp.where(component == 0, one, none)
        scale_a = jnp.where(among(4, 5, 6), -0.5 * one, scale_a)
        scale_a = jnp.where(among(7, 8, 9), -one, scale_a)
        scale_b = jnp.where(among(1, 2, 3), one, none)
        first = jnp.where(
            among(1, 4, 7, 8), kx, jnp.where(among(2, 5, 9), ky, jnp.where(among(3, 6), kz, one))
        )
        second = jnp.where(
            among(4), kx, jnp.where(among(5, 7), ky, jnp.where(among(6, 8, 9), kz, one))
        )
        return first * second * scale_a, first * scale_b

    room = (LANES - used) // 8
    amap[0], amap[1] = maps(jnp.where(lane < used, lane // 8, (lane - used) // 8))
    amap[2], amap[3] = maps(
        jnp.where(
            lane < used,
            lane // 8,
            jnp.where(lane < used + (MOM - room) * 8, room + (lane - used) // 8, MOM),
        )
    )

    for off in range(1, GROUP):
        copies[off - 1].wait_recv()
        rows[:, off * LANES : (off + 1) * LANES] = landed[off]

    tile = 16

    def make_trig(step, first, last):
        @pl.loop(first, last)
        def _(chunk):
            at = pl.multiple_of(chunk * tile, tile)
            phase = 0.0
            for axis in range(3):
                phase += wide(kmap[axis, pl.ds(at, tile)], GROUP) * rows[3 * step + axis, :][None]
            sine, cosine = sin_cos(phase)
            trig[step, 0, pl.ds(at, tile)] = cosine
            trig[step, 1, pl.ds(at, tile)] = sine
            high[step, 0, pl.ds(at, tile)], low[step, 0, pl.ds(at, tile)] = split(cosine)
            high[step, 1, pl.ds(at, tile)], low[step, 1, pl.ds(at, tile)] = split(sine)

    def along(at, rows_here, direction):
        out = 0.0
        for axis in range(3):
            out += wide(kmap[axis, pl.ds(at, rows_here)], GROUP) * direction(axis)
        return out

    def make_tangent(step, direction):
        @pl.loop(0, kdev // tile)
        def _(chunk):
            at = pl.multiple_of(chunk * tile, tile)
            k_dot_dir = along(at, tile, direction)
            for which in range(2):
                moved = k_dot_dir * trig[step, which, pl.ds(at, tile)]
                high[steps, which, pl.ds(at, tile)], low[steps, which, pl.ds(at, tile)] = split(
                    moved
                )

    def make_sums(source, slots):
        count = 2 * len(slots) * kdev
        here = pl.ds(source, len(slots))
        wide_sum = jnp.dot(
            high[here].reshape(count, atoms), w1[...], preferred_element_type=F32
        )
        rest = jnp.dot(
            low[here].reshape(count, atoms), w1[:, 0:LANES], preferred_element_type=F32
        )
        both = wide_sum[:, 0:LANES] + wide_sum[:, LANES:] + rest
        a, b = amap[0], amap[1]
        for place, slot in enumerate(slots):
            cos_sum = both[2 * place * kdev : (2 * place + 1) * kdev]
            sin_sum = both[(2 * place + 1) * kdev : (2 * place + 2) * kdev]
            sums[slot, 0] = spread(a * cos_sum - b * sin_sum)
            sums[slot, 1] = spread(a * sin_sum + b * cos_sum)

    def operand(real, imag):
        one = real * amap[0] + imag * amap[1]
        two = real * amap[2] + imag * amap[3]
        top = one.astype(BF16)
        rest = jnp.where(lane < used, one - top.astype(F32), two).astype(BF16)
        return jnp.concatenate([top, rest], axis=1)

    def project(first, second):
        both = jnp.concatenate([operand(*first), operand(*second)], axis=0)
        proj[...] = jnp.dot(both, w2[...], preferred_element_type=F32)

    def factor_part(step, slot):
        acc[3:9] = jnp.zeros((6, 8, atoms), F32)
        real, imag = sums[slot, 0], sums[slot, 1]
        project((real, imag), (imag, -real))

        @pl.loop(0, kdev // tile)
        def _(chunk):
            at = pl.multiple_of(chunk * tile, tile)
            value = (
                trig[step, 0, pl.ds(at, tile)] * proj[pl.ds(at, tile)]
                + trig[step, 1, pl.ds(at, tile)] * proj[pl.ds(pl.multiple_of(kdev + at, tile), tile)]
            )
            row = 3
            for axis in range(3):
                weighted = wide(kmap[3 + axis, pl.ds(at, tile)], GROUP) * value
                for other in range(axis, 3):
                    acc[row] += fold(wide(kmap[other, pl.ds(at, tile)], GROUP) * weighted)
                    row += 1

    def tangent_part(step, slot):
        acc[0:3] = jnp.zeros((3, 8, atoms), F32)
        real, imag = sums[slot, 0], sums[slot, 1]
        project((real, imag), (-imag, real))

        @pl.loop(0, kdev // tile)
        def _(chunk):
            at = pl.multiple_of(chunk * tile, tile)
            value = (
                trig[step, 0, pl.ds(at, tile)] * proj[pl.ds(at, tile)]
                - trig[step, 1, pl.ds(at, tile)] * proj[pl.ds(pl.multiple_of(kdev + at, tile), tile)]
            )
            for axis in range(3):
                acc[axis] += fold(wide(kmap[3 + axis, pl.ds(at, tile)], GROUP) * value)

    def send_force(step, direction):
        summed = [jnp.sum(acc[row], axis=0, keepdims=True) for row in range(9)]
        second = {}
        row = 3
        for axis in range(3):
            for other in range(axis, 3):
                second[axis, other] = second[other, axis] = summed[row]
                row += 1
        part[step] = jnp.zeros((GROUP, 8, LANES), F32)
        for axis in range(3):
            out = summed[axis]
            for other in range(3):
                out = out - second[axis, other] * direction(other)
            for off in range(GROUP):
                part[step, off, axis : axis + 1, :] = out[:, off * LANES : (off + 1) * LANES]
        started = []
        for over in range(kvecs):
            for off in range(GROUP):
                if over == 0 and off == 0:
                    continue
                started.append(
                    pltpu.make_async_remote_copy(
                        src_ref=part.at[step, off],
                        dst_ref=bricks.at[step, over, off],
                        send_sem=zsend_sem.at[step, over, off],
                        recv_sem=zrecv_sem.at[step, over, off],
                        device_id=(behind(off), lax.rem(mev + over, kvecs)),
                        device_id_type=MESH,
                    )
                )
                started[-1].start()
        return started

    def finish_force(step, started):
        for copy in started:
            copy.wait_recv()
        shares = []
        for over in range(kvecs):
            out = part[step, 0] if over == 0 else bricks[step, over, 0]
            for off in range(1, GROUP):
                out = out + bricks[step, over, off]
            shares.append(out)
        out = jnp.zeros((8, LANES), F32)
        for owner in range(kvecs):
            over = lax.rem(mev + kvecs - owner, kvecs)
            share = shares[0]
            for other in range(1, kvecs):
                share = jnp.where(over == other, shares[other], share)
            out = out + share
        return out[0:3]

    def first_direction(axis):
        return rows[3 * steps + axis, :][None]

    last = steps - 1
    chunks = kdev // tile
    make_trig(last, 0, chunks)
    make_tangent(last, first_direction)
    for off in range(1, GROUP):
        copies[GROUP - 1 + off - 1].wait_recv()
    moments = jnp.concatenate(
        [sent[:, pl.ds(me, 1)].reshape(used, LANES)]
        + [qall[off].reshape(used, LANES) for off in range(1, GROUP)],
        axis=1,
    )
    q_high, q_low = split(moments)
    turned = jnp.concatenate([moments, jnp.zeros((LANES - used, atoms), F32)], axis=0).T
    w1[:, 0:LANES], w1[:, LANES:] = split(turned)
    fits = LANES - used
    w2[0:used] = q_high
    w2[used:LANES] = q_low[0:fits]
    w2[LANES : LANES + used] = q_high
    w2[LANES + used : LANES + 2 * used - fits] = q_low[fits:]
    w2[LANES + 2 * used - fits :] = jnp.zeros((2 * LANES - (LANES + 2 * used - fits), atoms), BF16)

    adj, fma = adj_ref[...], fma_ref[...]
    direction = first_direction
    for step in reversed(range(steps)):
        if step == last:
            make_sums(step, (0, 1))
            factor_part(step, 0)
        else:
            make_sums(steps, (1,))
        tangent_part(step, 1)
        started = send_force(step, direction)
        if step > 0:
            make_trig(step - 1, 0, chunks)
        force = finish_force(step, started)
        adj = adj - time_step * force
        fma = fma + time_step * adj
        copies += started
        if step > 0:
            fresh[step - 1] = jnp.concatenate([fma * inv_mass, jnp.zeros((5, LANES), F32)], axis=0)
            sends = []
            for off in range(1, GROUP):
                sends.append(
                    brick_copy(
                        2 + steps + step - 1,
                        off,
                        fresh.at[step - 1],
                        flown.at[step - 1, off],
                        ahead(off),
                    )
                )
                sends[-1].start()
            dirs[step - 1, :, 0:LANES] = fresh[step - 1]
            make_sums(step - 1, (0,))
            factor_part(step - 1, 0)
            for off in range(1, GROUP):
                sends[off - 1].wait_recv()
                dirs[step - 1, :, off * LANES : (off + 1) * LANES] = flown[step - 1, off]
            copies += sends

            def direction(axis, step=step):
                return dirs[step - 1, axis, :][None]

            make_tangent(step - 1, direction)
    out_adj[...] = adj
    out_fma[...] = fma
    for copy in copies:
        copy.wait_send()


def fused(kvecs, bricks, positions, moments, adj_pos, final_momentum_adjoint, species, masses, kint):
    steps, _, here = positions.shape
    kdev = kint.shape[0]
    atoms = here * GROUP
    phases = 2 + 2 * steps - 1
    prefactor = energy_scale / math.sqrt(here * bricks)
    vmem = pl.BlockSpec(memory_space=pltpu.VMEM)
    small = jax.ShapeDtypeStruct((3, here), F32)
    return pl.pallas_call(
        functools.partial(kernel, kvecs, prefactor),
        out_shape=(small, small),
        in_specs=[vmem] * 5 + [pl.BlockSpec(memory_space=pltpu.SMEM), vmem],
        out_specs=(vmem, vmem),
        scratch_shapes=[
            pltpu.VMEM((16, here), F32),
            pltpu.VMEM((GROUP, 16, here), F32),
            pltpu.VMEM((steps, GROUP, 8, here), F32),
            pltpu.VMEM((16, atoms), F32),
            pltpu.VMEM((MOM, GROUP, 8, here), F32),
            pltpu.VMEM((GROUP, MOM, 8, here), F32),
            pltpu.VMEM((6, kdev, LANES), F32),
            pltpu.VMEM((4, kdev, LANES), F32),
            pltpu.VMEM((atoms, 2 * LANES), BF16),
            pltpu.VMEM((2 * LANES, atoms), BF16),
            pltpu.VMEM((steps, 2, kdev, atoms), F32),
            pltpu.VMEM((steps + 1, 2, kdev, atoms), BF16),
            pltpu.VMEM((steps + 1, 2, kdev, atoms), BF16),
            pltpu.VMEM((2, 2, kdev, LANES), F32),
            pltpu.VMEM((2 * kdev, atoms), F32),
            pltpu.VMEM((9, 8, atoms), F32),
            pltpu.VMEM((steps, GROUP, 8, here), F32),
            pltpu.VMEM((steps, kvecs, GROUP, 8, here), F32),
            pltpu.VMEM((steps, 8, here), F32),
            pltpu.VMEM((steps, 8, atoms), F32),
            pltpu.SemaphoreType.DMA((phases, GROUP)),
            pltpu.SemaphoreType.DMA((phases, GROUP)),
            pltpu.SemaphoreType.DMA((steps, kvecs, GROUP)),
            pltpu.SemaphoreType.DMA((steps, kvecs, GROUP)),
        ],
        compiler_params=pltpu.CompilerParams(
            collective_id=0, has_side_effects=True, vmem_limit_bytes=48 << 20
        ),
    )(
        positions,
        moments,
        adj_pos,
        final_momentum_adjoint,
        species.reshape(1, here),
        masses,
        kint,
    )


def solution(mesh):
    bricks, kvecs = mesh.shape["brick"], mesh.shape["kvec"]
    if bricks != GROUP:
        return plain(mesh)
    placed = (
        P(None, None, "brick"),
        P("brick", None),
        P(None, "brick"),
        P(None, "brick"),
        P("brick"),
        P(),
        P("kvec", None),
    )
    return jax.shard_map(
        functools.partial(fused, kvecs, bricks),
        mesh=mesh,
        in_specs=placed,
        out_specs=(P(None, "brick"), P(None, "brick")),
        check_vma=False,
    )
```

```python
import functools
import math

import jax
import jax.numpy as jnp
from jax import lax
from jax.experimental import pallas as pl
from jax.experimental.pallas import tpu as pltpu
from jax.sharding import PartitionSpec as P

exact = lax.Precision.HIGHEST
wavevector_scale = 0.5
time_step = 0.5
energy_scale = 0.125


def coef_arrays(wavevector_phase):
    kx, ky, kz = (wavevector_phase[:, 0], wavevector_phase[:, 1], wavevector_phase[:, 2])
    ones = jnp.ones_like(kx)
    zeros = jnp.zeros_like(kx)
    acoef = jnp.stack(
        [
            ones,
            zeros,
            zeros,
            zeros,
            -0.5 * kx * kx,
            -0.5 * ky * ky,
            -0.5 * kz * kz,
            -kx * ky,
            -kx * kz,
            -ky * kz,
        ],
        1,
    )
    bcoef = jnp.stack([zeros, kx, ky, kz, zeros, zeros, zeros, zeros, zeros, zeros], 1)
    return (acoef, bcoef)


def moment_sums(cos_w, sin_w, moments, acoef, bcoef):
    channels = moments.shape[1] // 10
    cos_part = jnp.dot(cos_w, moments, precision=exact).reshape(cos_w.shape[0], 10, channels)
    sine_component = jnp.dot(sin_w, moments, precision=exact).reshape(cos_w.shape[0], 10, channels)
    real_sum = jnp.einsum("km,kmc->kc", acoef, cos_part, precision=exact) - jnp.einsum(
        "km,kmc->kc", bcoef, sine_component, precision=exact
    )
    imag_sum = jnp.einsum("km,kmc->kc", acoef, sine_component, precision=exact) + jnp.einsum(
        "km,kmc->kc", bcoef, cos_part, precision=exact
    )
    return (real_sum, imag_sum)


def weave_terms(leading_dimension, trailing, acoef, bcoef):
    woven = (
        leading_dimension[:, None, :] * acoef[:, :, None] + trailing[:, None, :] * bcoef[:, :, None]
    )
    return woven.reshape(leading_dimension.shape[0], -1)


def tangent_force(
    wavevector_phase,
    k_weight,
    acoef,
    bcoef,
    factor,
    tangent,
    cosines,
    sines,
    k_dot_dir,
    moments,
    prefactor,
):
    factor_re, factor_im = factor
    tangent_re, tangent_im = tangent
    stacked = jnp.stack(
        [
            weave_terms(tangent_im, -tangent_re, acoef, bcoef),
            weave_terms(tangent_re, tangent_im, acoef, bcoef),
            weave_terms(factor_re, factor_im, acoef, bcoef),
            weave_terms(factor_im, -factor_re, acoef, bcoef),
        ]
    )
    projected = jnp.einsum("jkf,af->jka", stacked, moments, precision=exact)
    inner_sum = (
        cosines * projected[0]
        - sines * projected[1]
        - k_dot_dir * (cosines * projected[2] + sines * projected[3])
    )
    return jnp.dot((k_weight[:, None] * wavevector_phase).T, inner_sum, precision=exact) * prefactor


def plain_local(positions, moments, adj_pos, final_momentum_adjoint, species, masses, kint):
    wavevector_phase = kint.astype(jnp.float32) * wavevector_scale
    ksq = jnp.sum(wavevector_phase * wavevector_phase, 1)
    k_weight = jnp.exp(-ksq / 4.0) / jnp.maximum(ksq, 1.0)
    acoef, bcoef = coef_arrays(wavevector_phase)
    prefactor = energy_scale / math.sqrt(positions.shape[2] * lax.axis_size("brick"))
    onehot = (species[None, :] == jnp.arange(masses.shape[0], dtype=jnp.int32)[:, None]).astype(
        jnp.float32
    )
    inv_mass = jnp.dot(1.0 / masses, onehot, precision=exact)
    num_steps = positions.shape[0]

    def step_phases(step_index):
        phase = jnp.dot(wavevector_phase, positions[step_index], precision=exact)
        return (jnp.cos(phase), jnp.sin(phase))

    phase_list = [step_phases(step_index) for step_index in range(num_steps)]
    for step_index in reversed(range(num_steps)):
        cosines, sines = phase_list[step_index]
        direction = final_momentum_adjoint * inv_mass
        k_dot_dir = jnp.dot(wavevector_phase, direction, precision=exact)
        tangent_real_part, tan_im = moment_sums(
            k_dot_dir * cosines, k_dot_dir * sines, moments, acoef, bcoef
        )
        fac_re, fac_im = moment_sums(cosines, sines, moments, acoef, bcoef)
        summed_terms = lax.psum((fac_re, fac_im, -tan_im, tangent_real_part), "brick")
        factor = (summed_terms[0], summed_terms[1])
        tangent = (summed_terms[2], summed_terms[3])
        partial_force = tangent_force(
            wavevector_phase,
            k_weight,
            acoef,
            bcoef,
            factor,
            tangent,
            cosines,
            sines,
            k_dot_dir,
            moments,
            prefactor,
        )
        force = lax.psum(partial_force, "kvec")
        adj_pos = adj_pos - time_step * force
        final_momentum_adjoint = final_momentum_adjoint + time_step * adj_pos
    return (adj_pos, final_momentum_adjoint)


def plain(mesh):
    placed = (
        P(None, None, "brick"),
        P("brick", None),
        P(None, "brick"),
        P(None, "brick"),
        P("brick"),
        P(),
        P("kvec", None),
    )
    return jax.shard_map(
        plain_local,
        mesh=mesh,
        in_specs=placed,
        out_specs=(P(None, "brick"), P(None, "brick")),
        check_vma=False,
    )


MESH = pl.DeviceIdType.MESH
GROUP = 8
MOM = 10
LANES = 128
F32, BF16 = jnp.float32, jnp.bfloat16
two_over_pi = 2.0 / math.pi
half_pi_parts = (1.5703125, 4.837512969970703125e-4, 7.549789948768648e-8)


def sin_cos(phase):
    n = jnp.round(phase * two_over_pi)
    r = phase - n * half_pi_parts[0]
    r = r - n * half_pi_parts[1]
    r = r - n * half_pi_parts[2]
    q = n.astype(jnp.int32)
    z = r * r
    s = r + r * z * (-1.6666654611e-1 + z * (8.3321608736e-3 + z * -1.9515295891e-4))
    c = 1.0 - 0.5 * z + z * z * (
        4.166664568298827e-2 + z * (-1.388731625493765e-3 + z * 2.443315711809948e-5)
    )
    odd = (q & 1) == 1
    sine = jnp.where(odd, c, s)
    cosine = jnp.where(odd, s, c)
    sine = jnp.where((q & 2) == 2, -sine, sine)
    cosine = jnp.where(((q + 1) & 2) == 2, -cosine, cosine)
    return sine, cosine


def split(x):
    high = x.astype(BF16)
    return high, (x - high.astype(F32)).astype(BF16)


def wide(x, copies):
    return jnp.concatenate([x] * copies, axis=1)


def fold(x):
    out = x[0:8]
    for row in range(8, x.shape[0], 8):
        out = out + x[row : row + 8]
    return out


def spread(x):
    for shift in (8, 16, 32, 64):
        x = x + pltpu.roll(x, shift, 1)
    return x


def kernel(
    kvecs,
    prefactor,
    pos_ref,
    mom_hbm,
    adj_ref,
    fma_ref,
    spec_ref,
    mass_ref,
    kint_ref,
    out_adj,
    out_fma,
    mom_ref,
    mom_sem,
    pack,
    landed,
    flown,
    rows,
    sent,
    qall,
    kmap,
    amap,
    w1,
    w2,
    trig,
    high,
    low,
    sums,
    proj,
    acc,
    part,
    bricks,
    fresh,
    dirs,
    send_sem,
    recv_sem,
    zsend_sem,
    zrecv_sem,
):
    me = lax.axis_index("brick")
    mev = lax.axis_index("kvec")
    atoms = LANES * GROUP
    kdev = kint_ref.shape[0]
    steps = pos_ref.shape[0]

    def ahead(off):
        return lax.rem(me + off, GROUP)

    def behind(off):
        return lax.rem(me + GROUP - off, GROUP)

    def brick_copy(phase, off, src, dst, target):
        return pltpu.make_async_remote_copy(
            src_ref=src,
            dst_ref=dst,
            send_sem=send_sem.at[phase, off],
            recv_sem=recv_sem.at[phase, off],
            device_id=(target, mev),
            device_id_type=MESH,
        )

    fetch = pltpu.make_async_copy(mom_hbm, mom_ref, mom_sem)
    fetch.start()
    barrier = pltpu.get_barrier_semaphore()
    for over in range(kvecs):
        for off in range(GROUP):
            if over > 0 or off > 0:
                pl.semaphore_signal(
                    barrier,
                    inc=1,
                    device_id=(ahead(off), lax.rem(mev + over, kvecs)),
                    device_id_type=MESH,
                )

    species = spec_ref[...]
    mass = jnp.zeros(species.shape, F32)
    for kind in range(mass_ref.shape[0]):
        mass = jnp.where(species == kind, mass_ref[kind], mass)
    inv_mass = 1.0 / mass
    pack[...] = jnp.zeros_like(pack)
    for step in range(steps):
        pack[3 * step : 3 * step + 3, :] = pos_ref[step]
    pack[3 * steps : 3 * steps + 3, :] = fma_ref[...] * inv_mass
    fetch.wait()
    for piece in range(mom_ref.shape[1] // LANES):
        turned = mom_ref[:, piece * LANES : (piece + 1) * LANES].T
        sent[2 * piece : 2 * piece + 2] = turned.reshape(2, GROUP, 8, LANES)

    wave = kint_ref[...].astype(F32) * wavevector_scale
    kx = jnp.broadcast_to(wave[:, 0:1], (kdev, LANES))
    ky = jnp.broadcast_to(wave[:, 1:2], (kdev, LANES))
    kz = jnp.broadcast_to(wave[:, 2:3], (kdev, LANES))
    ksq = kx * kx + ky * ky + kz * kz
    weight = jnp.exp(-ksq / 4.0) / jnp.maximum(ksq, 1.0) * prefactor
    for axis, k in enumerate((kx, ky, kz)):
        kmap[axis] = k
        kmap[3 + axis] = weight * k
    lane = lax.broadcasted_iota(jnp.int32, (1, LANES), 1)
    used = MOM * 8

    def maps(component):
        def among(*names):
            out = component == names[0]
            for name in names[1:]:
                out = out | (component == name)
            return out

        one, none = jnp.ones((1, LANES), F32), jnp.zeros((1, LANES), F32)
        scale_a = jnp.where(component == 0, one, none)
        scale_a = jnp.where(among(4, 5, 6), -0.5 * one, scale_a)
        scale_a = jnp.where(among(7, 8, 9), -one, scale_a)
        scale_b = jnp.where(among(1, 2, 3), one, none)
        first = jnp.where(
            among(1, 4, 7, 8), kx, jnp.where(among(2, 5, 9), ky, jnp.where(among(3, 6), kz, one))
        )
        second = jnp.where(
            among(4), kx, jnp.where(among(5, 7), ky, jnp.where(among(6, 8, 9), kz, one))
        )
        return first * second * scale_a, first * scale_b

    room = (LANES - used) // 8
    amap[0], amap[1] = maps(jnp.where(lane < used, lane // 8, (lane - used) // 8))
    amap[2], amap[3] = maps(
        jnp.where(
            lane < used,
            lane // 8,
            jnp.where(lane < used + (MOM - room) * 8, room + (lane - used) // 8, MOM),
        )
    )

    pl.semaphore_wait(barrier, GROUP * kvecs - 1)
    copies = []
    for off in range(1, GROUP):
        copies.append(
            brick_copy(0, off, pack, landed.at[off], ahead(off))
        )
        copies[-1].start()
    for off in range(1, GROUP):
        copies.append(
            brick_copy(
                1,
                off,
                sent.at[:, ahead(off)],
                qall.at[off],
                ahead(off),
            )
        )
        copies[-1].start()
    rows[:, 0:LANES] = pack[...]

    for off in range(1, GROUP):
        copies[off - 1].wait_recv()
        rows[:, off * LANES : (off + 1) * LANES] = landed[off]

    tile = 16

    def make_trig(step, first, last):
        @pl.loop(first, last)
        def _(chunk):
            at = pl.multiple_of(chunk * tile, tile)
            phase = 0.0
            for axis in range(3):
                phase += wide(kmap[axis, pl.ds(at, tile)], GROUP) * rows[3 * step + axis, :][None]
            sine, cosine = sin_cos(phase)
            trig[step, 0, pl.ds(at, tile)] = cosine
            trig[step, 1, pl.ds(at, tile)] = sine
            high[step, 0, pl.ds(at, tile)], low[step, 0, pl.ds(at, tile)] = split(cosine)
            high[step, 1, pl.ds(at, tile)], low[step, 1, pl.ds(at, tile)] = split(sine)

    def along(at, rows_here, direction):
        out = 0.0
        for axis in range(3):
            out += wide(kmap[axis, pl.ds(at, rows_here)], GROUP) * direction(axis)
        return out

    def make_tangent(step, direction):
        @pl.loop(0, kdev // tile)
        def _(chunk):
            at = pl.multiple_of(chunk * tile, tile)
            k_dot_dir = along(at, tile, direction)
            for which in range(2):
                moved = k_dot_dir * trig[step, which, pl.ds(at, tile)]
                high[steps, which, pl.ds(at, tile)], low[steps, which, pl.ds(at, tile)] = split(
                    moved
                )

    def make_sums(source, slots):
        count = 2 * len(slots) * kdev
        here = pl.ds(source, len(slots))
        wide_sum = jnp.dot(
            high[here].reshape(count, atoms), w1[...], preferred_element_type=F32
        )
        rest = jnp.dot(
            low[here].reshape(count, atoms), w1[:, 0:LANES], preferred_element_type=F32
        )
        both = wide_sum[:, 0:LANES] + wide_sum[:, LANES:] + rest
        a, b = amap[0], amap[1]
        for place, slot in enumerate(slots):
            cos_sum = both[2 * place * kdev : (2 * place + 1) * kdev]
            sin_sum = both[(2 * place + 1) * kdev : (2 * place + 2) * kdev]
            sums[slot, 0] = spread(a * cos_sum - b * sin_sum)
            sums[slot, 1] = spread(a * sin_sum + b * cos_sum)

    def operand(real, imag):
        one = real * amap[0] + imag * amap[1]
        two = real * amap[2] + imag * amap[3]
        top = one.astype(BF16)
        rest = jnp.where(lane < used, one - top.astype(F32), two).astype(BF16)
        return jnp.concatenate([top, rest], axis=1)

    def project(first, second):
        both = jnp.concatenate([operand(*first), operand(*second)], axis=0)
        proj[...] = jnp.dot(both, w2[...], preferred_element_type=F32)

    def factor_part(step, slot):
        acc[3:9] = jnp.zeros((6, 8, atoms), F32)
        real, imag = sums[slot, 0], sums[slot, 1]
        project((real, imag), (imag, -real))

        @pl.loop(0, kdev // tile)
        def _(chunk):
            at = pl.multiple_of(chunk * tile, tile)
            value = (
                trig[step, 0, pl.ds(at, tile)] * proj[pl.ds(at, tile)]
                + trig[step, 1, pl.ds(at, tile)] * proj[pl.ds(pl.multiple_of(kdev + at, tile), tile)]
            )
            row = 3
            for axis in range(3):
                weighted = wide(kmap[3 + axis, pl.ds(at, tile)], GROUP) * value
                for other in range(axis, 3):
                    acc[row] += fold(wide(kmap[other, pl.ds(at, tile)], GROUP) * weighted)
                    row += 1

    def tangent_part(step, slot):
        acc[0:3] = jnp.zeros((3, 8, atoms), F32)
        real, imag = sums[slot, 0], sums[slot, 1]
        project((real, imag), (-imag, real))

        @pl.loop(0, kdev // tile)
        def _(chunk):
            at = pl.multiple_of(chunk * tile, tile)
            value = (
                trig[step, 0, pl.ds(at, tile)] * proj[pl.ds(at, tile)]
                - trig[step, 1, pl.ds(at, tile)] * proj[pl.ds(pl.multiple_of(kdev + at, tile), tile)]
            )
            for axis in range(3):
                acc[axis] += fold(wide(kmap[3 + axis, pl.ds(at, tile)], GROUP) * value)

    def send_force(step, direction):
        summed = [jnp.sum(acc[row], axis=0, keepdims=True) for row in range(9)]
        second = {}
        row = 3
        for axis in range(3):
            for other in range(axis, 3):
                second[axis, other] = second[other, axis] = summed[row]
                row += 1
        part[step] = jnp.zeros((GROUP, 4, LANES), F32)
        for axis in range(3):
            out = summed[axis]
            for other in range(3):
                out = out - second[axis, other] * direction(other)
            for off in range(GROUP):
                part[step, off, axis : axis + 1, :] = out[:, off * LANES : (off + 1) * LANES]
        started = []
        for over in reversed(range(kvecs)):
            for off in range(GROUP):
                if over == 0 and off == 0:
                    continue
                started.append(
                    pltpu.make_async_remote_copy(
                        src_ref=part.at[step, off],
                        dst_ref=bricks.at[step, over, off],
                        send_sem=zsend_sem.at[step, over, off],
                        recv_sem=zrecv_sem.at[step, over, off],
                        device_id=(behind(off), lax.rem(mev + over, kvecs)),
                        device_id_type=MESH,
                    )
                )
                started[-1].start()
        return started

    def finish_force(step, started):
        for copy in started:
            copy.wait_recv()
        shares = []
        for over in range(kvecs):
            out = part[step, 0] if over == 0 else bricks[step, over, 0]
            for off in range(1, GROUP):
                out = out + bricks[step, over, off]
            shares.append(out)
        out = jnp.zeros((4, LANES), F32)
        for owner in range(kvecs):
            over = lax.rem(mev + kvecs - owner, kvecs)
            share = shares[0]
            for other in range(1, kvecs):
                share = jnp.where(over == other, shares[other], share)
            out = out + share
        return out[0:3]

    def first_direction(axis):
        return rows[3 * steps + axis, :][None]

    last = steps - 1
    chunks = kdev // tile
    make_trig(last, 0, chunks)
    make_tangent(last, first_direction)
    for off in range(1, GROUP):
        copies[GROUP - 1 + off - 1].wait_recv()
    moments = jnp.concatenate(
        [sent[:, pl.ds(me, 1)].reshape(used, LANES)]
        + [qall[off].reshape(used, LANES) for off in range(1, GROUP)],
        axis=1,
    )
    q_high, q_low = split(moments)
    turned = jnp.concatenate([moments, jnp.zeros((LANES - used, atoms), F32)], axis=0).T
    w1[:, 0:LANES], w1[:, LANES:] = split(turned)
    fits = LANES - used
    w2[0:used] = q_high
    w2[used:LANES] = q_low[0:fits]
    w2[LANES : LANES + used] = q_high
    w2[LANES + used : LANES + 2 * used - fits] = q_low[fits:]
    w2[LANES + 2 * used - fits :] = jnp.zeros((2 * LANES - (LANES + 2 * used - fits), atoms), BF16)

    adj, fma = adj_ref[...], fma_ref[...]
    direction = first_direction
    for step in reversed(range(steps)):
        if step == last:
            make_sums(step, (0, 1))
            factor_part(step, 0)
        else:
            make_sums(steps, (1,))
        tangent_part(step, 1)
        started = send_force(step, direction)
        if step > 0:
            make_trig(step - 1, 0, chunks)
        force = finish_force(step, started)
        adj = adj - time_step * force
        fma = fma + time_step * adj
        copies += started
        if step > 0:
            fresh[step - 1] = jnp.concatenate([fma * inv_mass, jnp.zeros((5, LANES), F32)], axis=0)
            sends = []
            for off in range(1, GROUP):
                sends.append(
                    brick_copy(
                        2 + steps + step - 1,
                        off,
                        fresh.at[step - 1],
                        flown.at[step - 1, off],
                        ahead(off),
                    )
                )
                sends[-1].start()
            dirs[step - 1, :, 0:LANES] = fresh[step - 1]
            make_sums(step - 1, (0,))
            factor_part(step - 1, 0)
            for off in range(1, GROUP):
                sends[off - 1].wait_recv()
                dirs[step - 1, :, off * LANES : (off + 1) * LANES] = flown[step - 1, off]
            copies += sends

            def direction(axis, step=step):
                return dirs[step - 1, axis, :][None]

            make_tangent(step - 1, direction)
    out_adj[...] = adj
    out_fma[...] = fma
    for copy in copies:
        copy.wait_send()


def fused(kvecs, bricks, positions, moments, adj_pos, final_momentum_adjoint, species, masses, kint):
    steps, _, here = positions.shape
    kdev = kint.shape[0]
    atoms = here * GROUP
    phases = 2 + 2 * steps - 1
    prefactor = energy_scale / math.sqrt(here * bricks)
    vmem = pl.BlockSpec(memory_space=pltpu.VMEM)
    small = jax.ShapeDtypeStruct((3, here), F32)
    return pl.pallas_call(
        functools.partial(kernel, kvecs, prefactor),
        out_shape=(small, small),
        in_specs=[vmem, pl.BlockSpec(memory_space=pl.ANY)] + [vmem] * 3 + [pl.BlockSpec(memory_space=pltpu.SMEM), vmem],
        out_specs=(vmem, vmem),
        scratch_shapes=[
            pltpu.VMEM(moments.shape, F32),
            pltpu.SemaphoreType.DMA,
            pltpu.VMEM((16, here), F32),
            pltpu.VMEM((GROUP, 16, here), F32),
            pltpu.VMEM((steps, GROUP, 8, here), F32),
            pltpu.VMEM((16, atoms), F32),
            pltpu.VMEM((MOM, GROUP, 8, here), F32),
            pltpu.VMEM((GROUP, MOM, 8, here), F32),
            pltpu.VMEM((6, kdev, LANES), F32),
            pltpu.VMEM((4, kdev, LANES), F32),
            pltpu.VMEM((atoms, 2 * LANES), BF16),
            pltpu.VMEM((2 * LANES, atoms), BF16),
            pltpu.VMEM((steps, 2, kdev, atoms), F32),
            pltpu.VMEM((steps + 1, 2, kdev, atoms), BF16),
            pltpu.VMEM((steps + 1, 2, kdev, atoms), BF16),
            pltpu.VMEM((2, 2, kdev, LANES), F32),
            pltpu.VMEM((2 * kdev, atoms), F32),
            pltpu.VMEM((9, 8, atoms), F32),
            pltpu.VMEM((steps, GROUP, 4, here), F32),
            pltpu.VMEM((steps, kvecs, GROUP, 4, here), F32),
            pltpu.VMEM((steps, 8, here), F32),
            pltpu.VMEM((steps, 8, atoms), F32),
            pltpu.SemaphoreType.DMA((phases, GROUP)),
            pltpu.SemaphoreType.DMA((phases, GROUP)),
            pltpu.SemaphoreType.DMA((steps, kvecs, GROUP)),
            pltpu.SemaphoreType.DMA((steps, kvecs, GROUP)),
        ],
        compiler_params=pltpu.CompilerParams(
            collective_id=0, has_side_effects=True, vmem_limit_bytes=48 << 20
        ),
    )(
        positions,
        moments,
        adj_pos,
        final_momentum_adjoint,
        species.reshape(1, here),
        masses,
        kint,
    )


def solution(mesh):
    bricks, kvecs = mesh.shape["brick"], mesh.shape["kvec"]
    if bricks != GROUP:
        return plain(mesh)
    placed = (
        P(None, None, "brick"),
        P("brick", None),
        P(None, "brick"),
        P(None, "brick"),
        P("brick"),
        P(),
        P("kvec", None),
    )
    return jax.shard_map(
        functools.partial(fused, kvecs, bricks),
        mesh=mesh,
        in_specs=placed,
        out_specs=(P(None, "brick"), P(None, "brick")),
        check_vma=False,
    )
```

```python
import functools
import math

import jax
import jax.numpy as jnp
from jax import lax
from jax.experimental import pallas as pl
from jax.experimental.pallas import tpu as pltpu
from jax.sharding import PartitionSpec as P

exact = lax.Precision.HIGHEST
wavevector_scale = 0.5
time_step = 0.5
energy_scale = 0.125


def coef_arrays(wavevector_phase):
    kx, ky, kz = (wavevector_phase[:, 0], wavevector_phase[:, 1], wavevector_phase[:, 2])
    ones = jnp.ones_like(kx)
    zeros = jnp.zeros_like(kx)
    acoef = jnp.stack(
        [
            ones,
            zeros,
            zeros,
            zeros,
            -0.5 * kx * kx,
            -0.5 * ky * ky,
            -0.5 * kz * kz,
            -kx * ky,
            -kx * kz,
            -ky * kz,
        ],
        1,
    )
    bcoef = jnp.stack([zeros, kx, ky, kz, zeros, zeros, zeros, zeros, zeros, zeros], 1)
    return (acoef, bcoef)


def moment_sums(cos_w, sin_w, moments, acoef, bcoef):
    channels = moments.shape[1] // 10
    cos_part = jnp.dot(cos_w, moments, precision=exact).reshape(cos_w.shape[0], 10, channels)
    sine_component = jnp.dot(sin_w, moments, precision=exact).reshape(cos_w.shape[0], 10, channels)
    real_sum = jnp.einsum("km,kmc->kc", acoef, cos_part, precision=exact) - jnp.einsum(
        "km,kmc->kc", bcoef, sine_component, precision=exact
    )
    imag_sum = jnp.einsum("km,kmc->kc", acoef, sine_component, precision=exact) + jnp.einsum(
        "km,kmc->kc", bcoef, cos_part, precision=exact
    )
    return (real_sum, imag_sum)


def weave_terms(leading_dimension, trailing, acoef, bcoef):
    woven = (
        leading_dimension[:, None, :] * acoef[:, :, None] + trailing[:, None, :] * bcoef[:, :, None]
    )
    return woven.reshape(leading_dimension.shape[0], -1)


def tangent_force(
    wavevector_phase,
    k_weight,
    acoef,
    bcoef,
    factor,
    tangent,
    cosines,
    sines,
    k_dot_dir,
    moments,
    prefactor,
):
    factor_re, factor_im = factor
    tangent_re, tangent_im = tangent
    stacked = jnp.stack(
        [
            weave_terms(tangent_im, -tangent_re, acoef, bcoef),
            weave_terms(tangent_re, tangent_im, acoef, bcoef),
            weave_terms(factor_re, factor_im, acoef, bcoef),
            weave_terms(factor_im, -factor_re, acoef, bcoef),
        ]
    )
    projected = jnp.einsum("jkf,af->jka", stacked, moments, precision=exact)
    inner_sum = (
        cosines * projected[0]
        - sines * projected[1]
        - k_dot_dir * (cosines * projected[2] + sines * projected[3])
    )
    return jnp.dot((k_weight[:, None] * wavevector_phase).T, inner_sum, precision=exact) * prefactor


def plain_local(positions, moments, adj_pos, final_momentum_adjoint, species, masses, kint):
    wavevector_phase = kint.astype(jnp.float32) * wavevector_scale
    ksq = jnp.sum(wavevector_phase * wavevector_phase, 1)
    k_weight = jnp.exp(-ksq / 4.0) / jnp.maximum(ksq, 1.0)
    acoef, bcoef = coef_arrays(wavevector_phase)
    prefactor = energy_scale / math.sqrt(positions.shape[2] * lax.axis_size("brick"))
    onehot = (species[None, :] == jnp.arange(masses.shape[0], dtype=jnp.int32)[:, None]).astype(
        jnp.float32
    )
    inv_mass = jnp.dot(1.0 / masses, onehot, precision=exact)
    num_steps = positions.shape[0]

    def step_phases(step_index):
        phase = jnp.dot(wavevector_phase, positions[step_index], precision=exact)
        return (jnp.cos(phase), jnp.sin(phase))

    phase_list = [step_phases(step_index) for step_index in range(num_steps)]
    for step_index in reversed(range(num_steps)):
        cosines, sines = phase_list[step_index]
        direction = final_momentum_adjoint * inv_mass
        k_dot_dir = jnp.dot(wavevector_phase, direction, precision=exact)
        tangent_real_part, tan_im = moment_sums(
            k_dot_dir * cosines, k_dot_dir * sines, moments, acoef, bcoef
        )
        fac_re, fac_im = moment_sums(cosines, sines, moments, acoef, bcoef)
        summed_terms = lax.psum((fac_re, fac_im, -tan_im, tangent_real_part), "brick")
        factor = (summed_terms[0], summed_terms[1])
        tangent = (summed_terms[2], summed_terms[3])
        partial_force = tangent_force(
            wavevector_phase,
            k_weight,
            acoef,
            bcoef,
            factor,
            tangent,
            cosines,
            sines,
            k_dot_dir,
            moments,
            prefactor,
        )
        force = lax.psum(partial_force, "kvec")
        adj_pos = adj_pos - time_step * force
        final_momentum_adjoint = final_momentum_adjoint + time_step * adj_pos
    return (adj_pos, final_momentum_adjoint)


def plain(mesh):
    placed = (
        P(None, None, "brick"),
        P("brick", None),
        P(None, "brick"),
        P(None, "brick"),
        P("brick"),
        P(),
        P("kvec", None),
    )
    return jax.shard_map(
        plain_local,
        mesh=mesh,
        in_specs=placed,
        out_specs=(P(None, "brick"), P(None, "brick")),
        check_vma=False,
    )


MESH = pl.DeviceIdType.MESH
GROUP = 8
MOM = 10
LANES = 128
F32, BF16 = jnp.float32, jnp.bfloat16
two_over_pi = 2.0 / math.pi
half_pi_parts = (1.5703125, 4.837512969970703125e-4, 7.549789948768648e-8)


def sin_cos(phase):
    n = jnp.round(phase * two_over_pi)
    r = phase - n * half_pi_parts[0]
    r = r - n * half_pi_parts[1]
    r = r - n * half_pi_parts[2]
    q = n.astype(jnp.int32)
    z = r * r
    s = r + r * z * (-1.6666654611e-1 + z * (8.3321608736e-3 + z * -1.9515295891e-4))
    c = 1.0 - 0.5 * z + z * z * (
        4.166664568298827e-2 + z * (-1.388731625493765e-3 + z * 2.443315711809948e-5)
    )
    odd = (q & 1) == 1
    sine = jnp.where(odd, c, s)
    cosine = jnp.where(odd, s, c)
    sine = jnp.where((q & 2) == 2, -sine, sine)
    cosine = jnp.where(((q + 1) & 2) == 2, -cosine, cosine)
    return sine, cosine


def split(x):
    high = x.astype(BF16)
    return high, (x - high.astype(F32)).astype(BF16)


def wide(x, copies):
    return jnp.concatenate([x] * copies, axis=1)


def fold(x):
    out = x[0:8]
    for row in range(8, x.shape[0], 8):
        out = out + x[row : row + 8]
    return out


def spread(x):
    for shift in (8, 16, 32, 64):
        x = x + pltpu.roll(x, shift, 1)
    return x


def kernel(
    kvecs,
    prefactor,
    pos_ref,
    mom_hbm,
    adj_ref,
    fma_ref,
    spec_ref,
    mass_ref,
    kint_ref,
    out_adj,
    out_fma,
    mom_ref,
    mom_sem,
    pack,
    landed,
    flown,
    rows,
    sent,
    qall,
    kmap,
    amap,
    w1,
    w2,
    trig,
    high,
    low,
    sums,
    proj,
    acc,
    part,
    bricks,
    fresh,
    dirs,
    send_sem,
    recv_sem,
    zsend_sem,
    zrecv_sem,
):
    me = lax.axis_index("brick")
    mev = lax.axis_index("kvec")
    atoms = LANES * GROUP
    kdev = kint_ref.shape[0]
    steps = pos_ref.shape[0]

    def ahead(off):
        return lax.rem(me + off, GROUP)

    def behind(off):
        return lax.rem(me + GROUP - off, GROUP)

    def brick_copy(phase, off, src, dst, target):
        return pltpu.make_async_remote_copy(
            src_ref=src,
            dst_ref=dst,
            send_sem=send_sem.at[phase, off],
            recv_sem=recv_sem.at[phase, off],
            device_id=(target, mev),
            device_id_type=MESH,
        )

    fetch = pltpu.make_async_copy(mom_hbm, mom_ref, mom_sem)
    fetch.start()
    barrier = pltpu.get_barrier_semaphore()
    for over in range(kvecs):
        for off in range(GROUP):
            if over > 0 or off > 0:
                pl.semaphore_signal(
                    barrier,
                    inc=1,
                    device_id=(ahead(off), lax.rem(mev + over, kvecs)),
                    device_id_type=MESH,
                )

    species = spec_ref[...]
    mass = jnp.zeros(species.shape, F32)
    for kind in range(mass_ref.shape[0]):
        mass = jnp.where(species == kind, mass_ref[kind], mass)
    inv_mass = 1.0 / mass
    pack[...] = jnp.zeros_like(pack)
    for step in range(steps):
        pack[3 * step : 3 * step + 3, :] = pos_ref[step]
    pack[3 * steps : 3 * steps + 3, :] = fma_ref[...] * inv_mass
    fetch.wait()
    for piece in range(mom_ref.shape[1] // LANES):
        turned = mom_ref[:, piece * LANES : (piece + 1) * LANES].T
        sent[2 * piece : 2 * piece + 2] = turned.reshape(2, GROUP, 8, LANES)

    wave = kint_ref[...].astype(F32) * wavevector_scale
    kx = jnp.broadcast_to(wave[:, 0:1], (kdev, LANES))
    ky = jnp.broadcast_to(wave[:, 1:2], (kdev, LANES))
    kz = jnp.broadcast_to(wave[:, 2:3], (kdev, LANES))
    ksq = kx * kx + ky * ky + kz * kz
    weight = jnp.exp(-ksq / 4.0) / jnp.maximum(ksq, 1.0) * prefactor
    for axis, k in enumerate((kx, ky, kz)):
        kmap[axis] = k
        kmap[3 + axis] = weight * k
    lane = lax.broadcasted_iota(jnp.int32, (1, LANES), 1)
    used = MOM * 8

    def maps(component):
        def among(*names):
            out = component == names[0]
            for name in names[1:]:
                out = out | (component == name)
            return out

        one, none = jnp.ones((1, LANES), F32), jnp.zeros((1, LANES), F32)
        scale_a = jnp.where(component == 0, one, none)
        scale_a = jnp.where(among(4, 5, 6), -0.5 * one, scale_a)
        scale_a = jnp.where(among(7, 8, 9), -one, scale_a)
        scale_b = jnp.where(among(1, 2, 3), one, none)
        first = jnp.where(
            among(1, 4, 7, 8), kx, jnp.where(among(2, 5, 9), ky, jnp.where(among(3, 6), kz, one))
        )
        second = jnp.where(
            among(4), kx, jnp.where(among(5, 7), ky, jnp.where(among(6, 8, 9), kz, one))
        )
        return first * second * scale_a, first * scale_b

    room = (LANES - used) // 8
    amap[0], amap[1] = maps(jnp.where(lane < used, lane // 8, (lane - used) // 8))
    amap[2], amap[3] = maps(
        jnp.where(
            lane < used,
            lane // 8,
            jnp.where(lane < used + (MOM - room) * 8, room + (lane - used) // 8, MOM),
        )
    )

    pl.semaphore_wait(barrier, GROUP * kvecs - 1)
    copies = []
    for off in range(1, GROUP):
        copies.append(
            brick_copy(0, off, pack, landed.at[off], ahead(off))
        )
        copies[-1].start()
    for off in range(1, GROUP):
        copies.append(
            brick_copy(
                1,
                off,
                sent.at[:, ahead(off)],
                qall.at[off],
                ahead(off),
            )
        )
        copies[-1].start()
    rows[:, 0:LANES] = pack[...]

    for off in range(1, GROUP):
        copies[off - 1].wait_recv()
        rows[:, off * LANES : (off + 1) * LANES] = landed[off]

    tile = 16

    def make_trig(step, first, last):
        @pl.loop(first, last)
        def _(chunk):
            at = pl.multiple_of(chunk * tile, tile)
            phase = 0.0
            for axis in range(3):
                phase += wide(kmap[axis, pl.ds(at, tile)], GROUP) * rows[3 * step + axis, :][None]
            sine, cosine = sin_cos(phase)
            trig[step, 0, pl.ds(at, tile)] = cosine
            trig[step, 1, pl.ds(at, tile)] = sine
            high[step, 0, pl.ds(at, tile)], low[step, 0, pl.ds(at, tile)] = split(cosine)
            high[step, 1, pl.ds(at, tile)], low[step, 1, pl.ds(at, tile)] = split(sine)

    def along(at, rows_here, direction):
        out = 0.0
        for axis in range(3):
            out += wide(kmap[axis, pl.ds(at, rows_here)], GROUP) * direction(axis)
        return out

    def make_tangent(step, direction):
        @pl.loop(0, kdev // tile)
        def _(chunk):
            at = pl.multiple_of(chunk * tile, tile)
            k_dot_dir = along(at, tile, direction)
            for which in range(2):
                moved = k_dot_dir * trig[step, which, pl.ds(at, tile)]
                high[steps, which, pl.ds(at, tile)], low[steps, which, pl.ds(at, tile)] = split(
                    moved
                )

    def make_sums(source, slots):
        count = 2 * len(slots) * kdev
        here = pl.ds(source, len(slots))
        wide_sum = jnp.dot(
            high[here].reshape(count, atoms), w1[...], preferred_element_type=F32
        )
        rest = jnp.dot(
            low[here].reshape(count, atoms), w1[:, 0:LANES], preferred_element_type=F32
        )
        both = wide_sum[:, 0:LANES] + wide_sum[:, LANES:] + rest
        a, b = amap[0], amap[1]
        for place, slot in enumerate(slots):
            cos_sum = both[2 * place * kdev : (2 * place + 1) * kdev]
            sin_sum = both[(2 * place + 1) * kdev : (2 * place + 2) * kdev]
            sums[slot, 0] = spread(a * cos_sum - b * sin_sum)
            sums[slot, 1] = spread(a * sin_sum + b * cos_sum)

    def operand(real, imag):
        one = real * amap[0] + imag * amap[1]
        two = real * amap[2] + imag * amap[3]
        top = one.astype(BF16)
        rest = jnp.where(lane < used, one - top.astype(F32), two).astype(BF16)
        return jnp.concatenate([top, rest], axis=1)

    def project(first, second):
        both = jnp.concatenate([operand(*first), operand(*second)], axis=0)
        proj[...] = jnp.dot(both, w2[...], preferred_element_type=F32)

    span = 32

    def factor_part(step, slot):
        acc[3:9] = jnp.zeros((6, 8, atoms), F32)
        real, imag = sums[slot, 0], sums[slot, 1]
        project((real, imag), (imag, -real))

        @pl.loop(0, kdev // span)
        def _(chunk):
            at = pl.multiple_of(chunk * span, span)
            value = (
                trig[step, 0, pl.ds(at, span)] * proj[pl.ds(at, span)]
                + trig[step, 1, pl.ds(at, span)] * proj[pl.ds(pl.multiple_of(kdev + at, span), span)]
            )
            row = 3
            for axis in range(3):
                weighted = wide(kmap[3 + axis, pl.ds(at, span)], GROUP) * value
                for other in range(axis, 3):
                    acc[row] += fold(wide(kmap[other, pl.ds(at, span)], GROUP) * weighted)
                    row += 1

    def tangent_part(step, slot):
        acc[0:3] = jnp.zeros((3, 8, atoms), F32)
        real, imag = sums[slot, 0], sums[slot, 1]
        project((real, imag), (-imag, real))

        @pl.loop(0, kdev // span)
        def _(chunk):
            at = pl.multiple_of(chunk * span, span)
            value = (
                trig[step, 0, pl.ds(at, span)] * proj[pl.ds(at, span)]
                - trig[step, 1, pl.ds(at, span)] * proj[pl.ds(pl.multiple_of(kdev + at, span), span)]
            )
            for axis in range(3):
                acc[axis] += fold(wide(kmap[3 + axis, pl.ds(at, span)], GROUP) * value)

    def send_force(step, direction):
        summed = [jnp.sum(acc[row], axis=0, keepdims=True) for row in range(9)]
        second = {}
        row = 3
        for axis in range(3):
            for other in range(axis, 3):
                second[axis, other] = second[other, axis] = summed[row]
                row += 1
        part[step] = jnp.zeros((GROUP, 4, LANES), F32)
        for axis in range(3):
            out = summed[axis]
            for other in range(3):
                out = out - second[axis, other] * direction(other)
            for off in range(GROUP):
                part[step, off, axis : axis + 1, :] = out[:, off * LANES : (off + 1) * LANES]
        started = []
        for over in reversed(range(kvecs)):
            for off in range(GROUP):
                if over == 0 and off == 0:
                    continue
                started.append(
                    pltpu.make_async_remote_copy(
                        src_ref=part.at[step, off],
                        dst_ref=bricks.at[step, over, off],
                        send_sem=zsend_sem.at[step, over, off],
                        recv_sem=zrecv_sem.at[step, over, off],
                        device_id=(behind(off), lax.rem(mev + over, kvecs)),
                        device_id_type=MESH,
                    )
                )
                started[-1].start()
        return started

    def finish_force(step, started):
        for copy in started:
            copy.wait_recv()
        shares = []
        for over in range(kvecs):
            out = part[step, 0] if over == 0 else bricks[step, over, 0]
            for off in range(1, GROUP):
                out = out + bricks[step, over, off]
            shares.append(out)
        out = jnp.zeros((4, LANES), F32)
        for owner in range(kvecs):
            over = lax.rem(mev + kvecs - owner, kvecs)
            share = shares[0]
            for other in range(1, kvecs):
                share = jnp.where(over == other, shares[other], share)
            out = out + share
        return out[0:3]

    def first_direction(axis):
        return rows[3 * steps + axis, :][None]

    last = steps - 1
    chunks = kdev // tile
    make_trig(last, 0, chunks)
    make_tangent(last, first_direction)
    for off in range(1, GROUP):
        copies[GROUP - 1 + off - 1].wait_recv()
    moments = jnp.concatenate(
        [sent[:, pl.ds(me, 1)].reshape(used, LANES)]
        + [qall[off].reshape(used, LANES) for off in range(1, GROUP)],
        axis=1,
    )
    q_high, q_low = split(moments)
    turned = jnp.concatenate([moments, jnp.zeros((LANES - used, atoms), F32)], axis=0).T
    w1[:, 0:LANES], w1[:, LANES:] = split(turned)
    fits = LANES - used
    w2[0:used] = q_high
    w2[used:LANES] = q_low[0:fits]
    w2[LANES : LANES + used] = q_high
    w2[LANES + used : LANES + 2 * used - fits] = q_low[fits:]
    w2[LANES + 2 * used - fits :] = jnp.zeros((2 * LANES - (LANES + 2 * used - fits), atoms), BF16)

    adj, fma = adj_ref[...], fma_ref[...]
    direction = first_direction
    for step in reversed(range(steps)):
        if step == last:
            make_sums(step, (0, 1))
            factor_part(step, 0)
        else:
            make_sums(steps, (1,))
        tangent_part(step, 1)
        started = send_force(step, direction)
        if step > 0:
            make_trig(step - 1, 0, chunks)
        force = finish_force(step, started)
        adj = adj - time_step * force
        fma = fma + time_step * adj
        copies += started
        if step > 0:
            fresh[step - 1] = jnp.concatenate([fma * inv_mass, jnp.zeros((5, LANES), F32)], axis=0)
            sends = []
            for off in range(1, GROUP):
                sends.append(
                    brick_copy(
                        2 + steps + step - 1,
                        off,
                        fresh.at[step - 1],
                        flown.at[step - 1, off],
                        ahead(off),
                    )
                )
                sends[-1].start()
            dirs[step - 1, :, 0:LANES] = fresh[step - 1]
            make_sums(step - 1, (0,))
            factor_part(step - 1, 0)
            for off in range(1, GROUP):
                sends[off - 1].wait_recv()
                dirs[step - 1, :, off * LANES : (off + 1) * LANES] = flown[step - 1, off]
            copies += sends

            def direction(axis, step=step):
                return dirs[step - 1, axis, :][None]

            make_tangent(step - 1, direction)
    out_adj[...] = adj
    out_fma[...] = fma
    for copy in copies:
        copy.wait_send()


def fused(kvecs, bricks, positions, moments, adj_pos, final_momentum_adjoint, species, masses, kint):
    steps, _, here = positions.shape
    kdev = kint.shape[0]
    atoms = here * GROUP
    phases = 2 + 2 * steps - 1
    prefactor = energy_scale / math.sqrt(here * bricks)
    vmem = pl.BlockSpec(memory_space=pltpu.VMEM)
    small = jax.ShapeDtypeStruct((3, here), F32)
    return pl.pallas_call(
        functools.partial(kernel, kvecs, prefactor),
        out_shape=(small, small),
        in_specs=[vmem, pl.BlockSpec(memory_space=pl.ANY)] + [vmem] * 3 + [pl.BlockSpec(memory_space=pltpu.SMEM), vmem],
        out_specs=(vmem, vmem),
        scratch_shapes=[
            pltpu.VMEM(moments.shape, F32),
            pltpu.SemaphoreType.DMA,
            pltpu.VMEM((16, here), F32),
            pltpu.VMEM((GROUP, 16, here), F32),
            pltpu.VMEM((steps, GROUP, 8, here), F32),
            pltpu.VMEM((16, atoms), F32),
            pltpu.VMEM((MOM, GROUP, 8, here), F32),
            pltpu.VMEM((GROUP, MOM, 8, here), F32),
            pltpu.VMEM((6, kdev, LANES), F32),
            pltpu.VMEM((4, kdev, LANES), F32),
            pltpu.VMEM((atoms, 2 * LANES), BF16),
            pltpu.VMEM((2 * LANES, atoms), BF16),
            pltpu.VMEM((steps, 2, kdev, atoms), F32),
            pltpu.VMEM((steps + 1, 2, kdev, atoms), BF16),
            pltpu.VMEM((steps + 1, 2, kdev, atoms), BF16),
            pltpu.VMEM((2, 2, kdev, LANES), F32),
            pltpu.VMEM((2 * kdev, atoms), F32),
            pltpu.VMEM((9, 8, atoms), F32),
            pltpu.VMEM((steps, GROUP, 4, here), F32),
            pltpu.VMEM((steps, kvecs, GROUP, 4, here), F32),
            pltpu.VMEM((steps, 8, here), F32),
            pltpu.VMEM((steps, 8, atoms), F32),
            pltpu.SemaphoreType.DMA((phases, GROUP)),
            pltpu.SemaphoreType.DMA((phases, GROUP)),
            pltpu.SemaphoreType.DMA((steps, kvecs, GROUP)),
            pltpu.SemaphoreType.DMA((steps, kvecs, GROUP)),
        ],
        compiler_params=pltpu.CompilerParams(
            collective_id=0, has_side_effects=True, vmem_limit_bytes=48 << 20
        ),
    )(
        positions,
        moments,
        adj_pos,
        final_momentum_adjoint,
        species.reshape(1, here),
        masses,
        kint,
    )


def solution(mesh):
    bricks, kvecs = mesh.shape["brick"], mesh.shape["kvec"]
    if bricks != GROUP:
        return plain(mesh)
    placed = (
        P(None, None, "brick"),
        P("brick", None),
        P(None, "brick"),
        P(None, "brick"),
        P("brick"),
        P(),
        P("kvec", None),
    )
    return jax.shard_map(
        functools.partial(fused, kvecs, bricks),
        mesh=mesh,
        in_specs=placed,
        out_specs=(P(None, "brick"), P(None, "brick")),
        check_vma=False,
    )
```
